256 devices in a mesh: chan: 16 (over z, x_lo), win: 16 (over x_hi, y, core).
Axes of the slice: x: 4 (x_hi: 2, x_lo: 2; x = x_hi * 2 + x_lo), y: 4, z: 8, core: 2. Of those that a mesh axis runs over, the one named last changes fastest.
Arguments:
- records: bfloat16 [512, 128, 2048], P('win', None, 'chan'), may hold values from -8 to 8
- fir_taps: float32 [64], replicated, may hold values from -0.75 to 0.75
Outputs:
- correlations: bfloat16 [128, 128, 1024], P('chan', 'win')
The draws below stay inside these ranges and needn't reach their ends.
All inputs are finite; a program needn't handle non-finite values.
Results may differ from the reference program's by a relative error of at most 0.0038.
Values may be sent and summed in bfloat16 or wider, within the bound.
No kernel may reach another device: no remote copies, remote signals or barrier semaphores. Data moves between devices by JAX's collectives and lax.ppermute only.
A program may use at most 64 MiB of HBM per device.

```python
import math
import jax
import jax.numpy as jnp
from jax import lax

WINDOW_LEN = 2048
BAND = 512
FIRST_BIN = 16
LAGS = 512
HALF_WIDTH = 32
TAPS = 64
CHANNELS = 128
WINDOWS = 512


def draw_records(key, part):
    key_delay = jax.random.fold_in(key, 11)
    key_noise = jax.random.fold_in(key, 12)
    key_source = jax.random.fold_in(key, 13)
    delays = jax.random.randint(key_delay, (CHANNELS,), 0, LAGS)
    noise = jnp.clip(jax.random.normal(key_noise, (WINDOWS, CHANNELS, WINDOW_LEN), jnp.float32), -4.0, 4.0)
    source = jnp.clip(jax.random.normal(key_source, (WINDOWS, WINDOW_LEN), jnp.float32), -4.0, 4.0)
    sample_pos = jnp.mod(jnp.arange(WINDOW_LEN, dtype=jnp.int32)[None, :] - delays[:, None], WINDOW_LEN)
    shifted = source[:, sample_pos]
    return (noise + shifted).astype(jnp.bfloat16)


def gaussian(key, dims, scale, reach, kind=jnp.bfloat16):
    return jnp.clip(scale * jax.random.normal(key, dims, jnp.float32), -reach, reach).astype(kind)


def setup_inputs(seed: int = 0) -> dict:
    key_of = jax.random.split(jax.random.key(seed), 3)
    records = draw_records(jax.random.fold_in(key_of[2], 71), 0)
    fir_taps = gaussian(key_of[1], (TAPS,), TAPS ** -0.5, 0.75, jnp.float32)
    return {"records": records, "fir_taps": fir_taps}


def phase_angles(rows, cols, length):
    product = jnp.mod(rows[:, None] * cols[None, :], length)
    return 2.0 * math.pi / length * product.astype(jnp.float32)

def smoother_matrix():
    ramp = jnp.arange(BAND, dtype=jnp.int32)
    offset = jnp.mod(ramp[:, None] - ramp[None, :], BAND)
    near = (offset <= HALF_WIDTH) | (offset >= BAND - HALF_WIDTH)
    return near.astype(jnp.float32)

def reference(records, fir_taps):
    spectra = jnp.fft.rfft(records.astype(jnp.float32), axis=-1)[..., FIRST_BIN:FIRST_BIN + BAND]
    padded = jnp.zeros((WINDOW_LEN,), jnp.float32).at[:TAPS].set(fir_taps)
    response = jnp.fft.rfft(padded)[FIRST_BIN:FIRST_BIN + BAND]
    filtered = spectra * response
    filt_re = jnp.real(filtered)
    filt_im = jnp.imag(filtered)
    power_sum = filt_re * filt_re + filt_im * filt_im
    smooth = jnp.einsum('wcf,fg->wcg', power_sum, smoother_matrix(), precision=lax.Precision.HIGHEST) / (2 * HALF_WIDTH + 1)
    inv_amp = 1.0 / jnp.sqrt(smooth + 1e-06)
    white_re = (filt_re * inv_amp).astype(jnp.bfloat16).astype(jnp.float32)
    white_im = (filt_im * inv_amp).astype(jnp.bfloat16).astype(jnp.float32)
    cross_re = jnp.einsum('wif,wjf->ijf', white_re, white_re) + jnp.einsum('wif,wjf->ijf', white_im, white_im)
    cross_im = jnp.einsum('wif,wjf->ijf', white_im, white_re) - jnp.einsum('wif,wjf->ijf', white_re, white_im)
    band_bins = FIRST_BIN + jnp.arange(BAND, dtype=jnp.int32)
    lag_steps = jnp.arange(2 * LAGS, dtype=jnp.int32) - LAGS
    angles = phase_angles(band_bins, lag_steps, WINDOW_LEN)
    inverse = jnp.concatenate([jnp.cos(angles), -jnp.sin(angles)], axis=0) / (WINDOWS * BAND)
    stacked = jnp.concatenate([cross_re, cross_im], axis=-1).reshape(CHANNELS * CHANNELS, 2 * BAND)
    lagged = jnp.dot(stacked, inverse, precision=lax.Precision.HIGHEST, preferred_element_type=jnp.float32)
    return lagged.reshape(CHANNELS, CHANNELS, 2 * LAGS).astype(jnp.bfloat16)
```

```python
import functools
import math

import jax
import jax.numpy as jnp
import ml_dtypes
import numpy as np
from jax import lax
from jax.experimental import pallas as pl
from jax.experimental.pallas import tpu as pltpu
from jax.sharding import PartitionSpec as P

LENGTH = 2048
BAND = 512
FIRST_BIN = 16
LAGS = 512
HALF_WIDTH = 32
TAPS = 64
CHANNELS = 128
WINDOWS = 512
BOTH = ("chan", "win")

BF16 = jnp.bfloat16
F32 = jnp.float32


def split_table(table):
    hi = table.astype(ml_dtypes.bfloat16)
    lo = (table - hi.astype(np.float64)).astype(ml_dtypes.bfloat16)
    return hi, lo


def phases(rows, cols):
    return 2.0 * math.pi / LENGTH * np.mod(rows[:, None] * cols[None, :], LENGTH).astype(np.float64)


@functools.cache
def tables():
    bins = FIRST_BIN + np.arange(BAND)
    angles = phases(bins, np.arange(LENGTH))
    forward = np.concatenate([np.cos(angles), -np.sin(angles)], axis=0)
    offset = np.mod(np.arange(BAND)[:, None] - np.arange(BAND)[None, :], BAND)
    near = (offset <= HALF_WIDTH) | (offset >= BAND - HALF_WIDTH)
    angles = phases(bins, np.arange(2 * LAGS) - LAGS)
    inverse = np.stack([np.cos(angles), -np.sin(angles)], axis=1) / (WINDOWS * BAND)
    inverse = inverse.reshape(BAND // 2, 2, 2, 2 * LAGS).transpose(1, 0, 2, 3).reshape(2 * BAND, 2 * LAGS)
    taps = forward[:, :TAPS].astype(np.float32)
    return split_table(forward), near.astype(ml_dtypes.bfloat16), split_table(inverse), taps


def dot_nt(a, b):
    return lax.dot_general(a, b, (((1,), (1,)), ((), ())), preferred_element_type=F32)


def dot_tn(a, b):
    return lax.dot_general(a, b, (((0,), (0,)), ((), ())), preferred_element_type=F32)


def dot_nn(a, b):
    return jnp.dot(a, b, preferred_element_type=F32)


def swap_halves(low, high, bit, shift, axis):
    size = low.shape[axis]
    new_low = jnp.where(bit, pltpu.roll(high, shift, axis), low)
    new_high = jnp.where(bit, high, pltpu.roll(low, size - shift, axis))
    return new_low, new_high


def whiten_kernel(y_ref, hi_ref, lo_ref, resp_ref, near_ref, out_ref, acc_ref):
    step = pl.program_id(0)
    blocks = y_ref.shape[0]
    x = jnp.concatenate([y_ref[s] for s in range(blocks)], axis=1)
    part = dot_nt(hi_ref[...], x) + dot_nt(lo_ref[...], x)

    @pl.when(step == 0)
    def _():
        acc_ref[...] = part

    @pl.when(step > 0)
    def _():
        acc_ref[...] += part

    @pl.when(step == pl.num_programs(0) - 1)
    def _():
        resp_re = jnp.concatenate([resp_ref[:BAND]] * 2, axis=1)
        resp_im = jnp.concatenate([resp_ref[BAND:]] * 2, axis=1)
        spec_re = acc_ref[:BAND]
        spec_im = acc_ref[BAND:]
        filt_re = spec_re * resp_re - spec_im * resp_im
        filt_im = spec_re * resp_im + spec_im * resp_re
        power = filt_re * filt_re + filt_im * filt_im
        first = power.astype(BF16)
        rest = power - first.astype(F32)
        second = rest.astype(BF16)
        third = (rest - second.astype(F32)).astype(BF16)
        near = near_ref[...]
        smooth = (dot_nn(near, first) + dot_nn(near, second) + dot_nn(near, third)) / (2 * HALF_WIDTH + 1)
        inv_amp = 1.0 / jnp.sqrt(smooth + 1e-06)
        white_re = filt_re * inv_amp
        white_im = filt_im * inv_amp
        half = CHANNELS
        a = [white_re[:, :half], white_re[:, half:], white_im[:, :half], white_im[:, half:]]
        row = lax.broadcasted_iota(jnp.int32, a[0].shape, 0)
        top = (row & 4) != 0
        mid = (row & 2) != 0
        for k in (0, 1):
            a[k], a[k + 2] = swap_halves(a[k], a[k + 2], top, 4, 0)
        for k in (0, 2):
            a[k], a[k + 1] = swap_halves(a[k], a[k + 1], mid, 2, 0)
        for k in range(4):
            out_ref[:, k] = a[k].reshape(BAND // 8, 8, CHANNELS).astype(BF16)


def cross_kernel(b_ref, out_ref):
    b = b_ref[...]
    wide = b.astype(F32)
    rows = wide.shape[0]
    row = lax.broadcasted_iota(jnp.int32, wide.shape, 0)
    imag = (row & 4) != 0
    odd = (row & 1) != 0
    turned = jnp.where(imag, pltpu.roll(wide, 4, 0), -pltpu.roll(wide, rows - 4, 0))
    zero = jnp.zeros_like(wide)
    columns = [
        jnp.where(odd, zero, wide),
        jnp.where(odd, wide, zero),
        jnp.where(odd, zero, turned),
        jnp.where(odd, turned, zero),
    ]
    z = jnp.concatenate([c.astype(BF16) for c in columns], axis=1)
    cross = dot_tn(b, z)
    row = lax.broadcasted_iota(jnp.int32, (CHANNELS, CHANNELS), 0)
    lane = lax.broadcasted_iota(jnp.int32, (CHANNELS, CHANNELS), 1)
    parts = [cross[:, k * CHANNELS : (k + 1) * CHANNELS] for k in range(4)]
    for down, right in ((4, 32), (2, 16), (1, 8)):
        row_bit = (row & down) != 0
        lane_bit = (lane & right) != 0
        for k in range(4):
            a = parts[k]
            up = pltpu.roll(pltpu.roll(a, CHANNELS - down, 0), right, 1)
            dn = pltpu.roll(pltpu.roll(a, down, 0), CHANNELS - right, 1)
            parts[k] = jnp.where(row_bit == lane_bit, a, jnp.where(row_bit, dn, up))
    lane_bit = (lane & 64) != 0
    for part in range(2):
        even, odd = swap_halves(parts[2 * part], parts[2 * part + 1], lane_bit, 64, 1)
        for high, a in enumerate((even, odd)):
            for c in range(CHANNELS // 8):
                start = c * 32 + high * 16 + part
                out_ref[pl.ds(start, 8, stride=2), :] = a[c * 8 : c * 8 + 8]


def lag_kernel(c_ref, hi_ref, lo_ref, out_ref):
    turned = c_ref[...].T
    lhs = jnp.concatenate([turned[:64], turned[64:]], axis=1)
    hi = lhs.astype(BF16)
    lo = (lhs - hi.astype(F32)).astype(BF16)
    total = dot_nn(hi, hi_ref[...]) + (dot_nn(lo, hi_ref[...]) + dot_nn(hi, lo_ref[...]))
    out_ref[...] = total.astype(BF16)


def body(records, fir_taps):
    (fwd_hi, fwd_lo), near, (inv_hi, inv_lo), taps_table = tables()
    y = lax.all_to_all(records, "chan", 0, 0, tiled=True)
    blocks = LENGTH // CHANNELS
    y = y.reshape(blocks, 2 * CHANNELS, CHANNELS)
    response = jnp.dot(
        taps_table,
        jnp.broadcast_to(fir_taps[:, None], (TAPS, 128)),
        precision=lax.Precision.HIGHEST,
        preferred_element_type=F32,
    )
    steps = 4
    depth = LENGTH // steps
    white = pl.pallas_call(
        whiten_kernel,
        grid=(steps,),
        in_specs=[
            pl.BlockSpec((blocks // steps, 2 * CHANNELS, CHANNELS), lambda s: (s, 0, 0)),
            pl.BlockSpec((2 * BAND, depth), lambda s: (0, s)),
            pl.BlockSpec((2 * BAND, depth), lambda s: (0, s)),
            pl.BlockSpec((2 * BAND, 128), lambda s: (0, 0)),
            pl.BlockSpec((BAND, BAND), lambda s: (0, 0)),
        ],
        out_specs=pl.BlockSpec((BAND // 8, 4, 8, CHANNELS), lambda s: (0, 0, 0, 0)),
        out_shape=jax.ShapeDtypeStruct((BAND // 8, 4, 8, CHANNELS), BF16),
        scratch_shapes=[pltpu.VMEM((2 * BAND, 2 * CHANNELS), F32)],
        name="whiten",
    )(y, fwd_hi, fwd_lo, response, near)
    owners = BAND // 2
    white = lax.all_to_all(white.reshape(owners, 8, CHANNELS), BOTH, 0, 0, tiled=True)
    cross = pl.pallas_call(
        cross_kernel,
        out_shape=jax.ShapeDtypeStruct((2 * owners, 128), F32),
        name="cross",
    )(white.reshape(owners * 8, CHANNELS))
    cross = lax.all_to_all(cross.reshape(owners, 2, 128), BOTH, 0, 0, tiled=True)
    lagged = pl.pallas_call(
        lag_kernel,
        out_shape=jax.ShapeDtypeStruct((64, 2 * LAGS), BF16),
        name="lag",
    )(cross.reshape(2 * owners, 128), inv_hi, inv_lo)
    return lagged.reshape(8, 8, 2 * LAGS)


def solution(mesh):
    in_specs = (P("win", None, "chan"), P())
    out_specs = P("chan", "win", None)
    return jax.shard_map(body, mesh=mesh, in_specs=in_specs, out_specs=out_specs, check_vma=False)
```

```python
import functools
import math

import jax
import jax.numpy as jnp
import ml_dtypes
import numpy as np
from jax import lax
from jax.experimental import pallas as pl
from jax.experimental.pallas import tpu as pltpu
from jax.sharding import PartitionSpec as P

LENGTH = 2048
BAND = 512
FIRST_BIN = 16
LAGS = 512
HALF_WIDTH = 32
TAPS = 64
CHANNELS = 128
WINDOWS = 512
BOTH = ("chan", "win")
RADIX = 4
QUARTER = LENGTH // RADIX
PER_CLASS = BAND // RADIX

BF16 = jnp.bfloat16
F32 = jnp.float32


def split_table(table):
    hi = table.astype(ml_dtypes.bfloat16)
    lo = (table - hi.astype(np.float64)).astype(ml_dtypes.bfloat16)
    return hi, lo


def phases(rows, cols):
    return 2.0 * math.pi / LENGTH * np.mod(rows[:, None] * cols[None, :], LENGTH).astype(np.float64)


@functools.cache
def tables():
    order = (RADIX * np.arange(PER_CLASS)[None, :] + np.arange(RADIX)[:, None]).reshape(-1)
    bins = FIRST_BIN + order
    cos, sin = (f(phases(bins, np.arange(QUARTER))).reshape(RADIX, PER_CLASS, QUARTER) for f in (np.cos, np.sin))
    even = [np.concatenate([cos[r], -sin[r]]) for r in (0, 2)]
    odd = np.concatenate(
        [
            np.concatenate([np.concatenate([cos[r], -s * sin[r]], axis=1), np.concatenate([-sin[r], -s * cos[r]], axis=1)])
            for r, s in ((1, 1), (3, -1))
        ]
    )
    forward = [np.concatenate(split_table(t)) for t in (*even, odd)]
    offset = np.mod(order[:, None] - order[None, :], BAND)
    near = (offset <= HALF_WIDTH) | (offset >= BAND - HALF_WIDTH)
    angles = phases(bins, np.arange(TAPS))
    taps = np.concatenate([np.cos(angles), -np.sin(angles)]).astype(np.float32)
    owned = order.reshape(2, 2, PER_CLASS).transpose(1, 0, 2).reshape(-1)
    angles = phases(FIRST_BIN + owned, np.arange(2 * LAGS) - LAGS)
    inverse = np.stack([np.cos(angles), -np.sin(angles)], axis=1) / (WINDOWS * BAND)
    return forward, near.astype(ml_dtypes.bfloat16), split_table(inverse.reshape(2 * BAND, 2 * LAGS)), taps


def dot_nt(a, b):
    return lax.dot_general(a, b, (((1,), (1,)), ((), ())), preferred_element_type=F32)


def dot_tn(a, b):
    return lax.dot_general(a, b, (((0,), (0,)), ((), ())), preferred_element_type=F32)


def dot_nn(a, b):
    return jnp.dot(a, b, preferred_element_type=F32)


def two_terms(x):
    hi = x.astype(BF16)
    return hi, (x - hi.astype(F32)).astype(BF16)


def swap_halves(low, high, bit, shift, axis):
    size = low.shape[axis]
    new_low = jnp.where(bit, pltpu.roll(high, shift, axis), low)
    new_high = jnp.where(bit, high, pltpu.roll(low, size - shift, axis))
    return new_low, new_high


def whiten_kernel(
    y_ref, odd_ref, even_hbm, half_hbm, near_hbm, resp_hbm, out_ref, even_ref, half_ref, near_ref, resp_ref, sems
):
    pairs = ((even_hbm, even_ref), (half_hbm, half_ref), (resp_hbm, resp_ref), (near_hbm, near_ref))
    copies = [pltpu.make_async_copy(src, dst, sems.at[k]) for k, (src, dst) in enumerate(pairs)]
    for copy in copies:
        copy.start()
    blocks = y_ref.shape[0] // RADIX
    sums = [[], [], [], []]
    for j in range(blocks):
        u = [y_ref[h * blocks + j].astype(F32) for h in range(RADIX)]
        even, odd = u[0] + u[2], u[1] + u[3]
        for k, x in enumerate((even + odd, even - odd, u[0] - u[2], u[1] - u[3])):
            sums[k].append(two_terms(x))
    terms = [[jnp.concatenate([x[t] for x in s], axis=1) for t in range(2)] for s in sums]
    inputs = [terms[0], terms[1], [jnp.concatenate([terms[2][t], terms[3][t]], axis=1) for t in range(2)]]
    spec = []
    for k, ref in enumerate((even_ref, half_ref, odd_ref)):
        hi, lo = inputs[k]
        rows = ref.shape[0] // 2
        if k < 2:
            copies[k].wait()
        both = dot_nt(ref[...], hi)
        spec.append(both[:rows] + both[rows:] + dot_nt(ref[:rows], lo))
    copies[2].wait()
    copies[3].wait()
    m = PER_CLASS
    spec_re = jnp.concatenate([spec[0][:m], spec[2][:m], spec[1][:m], spec[2][2 * m : 3 * m]])
    spec_im = jnp.concatenate([spec[0][m:], spec[2][m : 2 * m], spec[1][m:], spec[2][3 * m :]])
    resp_re = jnp.concatenate([resp_ref[:BAND]] * 2, axis=1)
    resp_im = jnp.concatenate([resp_ref[BAND:]] * 2, axis=1)
    filt_re = spec_re * resp_re - spec_im * resp_im
    filt_im = spec_re * resp_im + spec_im * resp_re
    power = filt_re * filt_re + filt_im * filt_im
    first = power.astype(BF16)
    second, third = two_terms(power - first.astype(F32))
    near = near_ref[...]
    smooth = (dot_nn(near, first) + dot_nn(near, second) + dot_nn(near, third)) * (1.0 / (2 * HALF_WIDTH + 1))
    inv_amp = lax.rsqrt(smooth + 1e-06)
    white = (filt_re * inv_amp, filt_im * inv_amp)
    row = lax.broadcasted_iota(jnp.int32, (m, CHANNELS), 0)
    bits = [(row & s) != 0 for s in (4, 2, 1)]
    for high in range(2):
        a = []
        for k in range(8):
            r = 2 * high + k // 4
            w = k % 2
            a.append(white[k // 2 % 2][r * m : (r + 1) * m, w * CHANNELS : (w + 1) * CHANNELS])
        for bit, shift in zip(bits, (4, 2, 1)):
            for k in range(8):
                if not k & shift:
                    a[k], a[k | shift] = swap_halves(a[k], a[k | shift], bit, shift, 0)
        for k in range(8):
            out_ref[high, :, k] = a[k].reshape(m // 8, 8, CHANNELS).astype(BF16)


def cross_kernel(b_ref, out_ref):
    wide = b_ref[...].astype(F32)
    first, second = wide[:, :8], wide[:, 8:]
    bit = (lax.broadcasted_iota(jnp.int32, first.shape, 1) & 4) != 0
    imag = (lax.broadcasted_iota(jnp.int32, first.shape, 1) & 2) != 0
    parts = []
    for x in swap_halves(first, second, bit, 4, 1):
        turned = jnp.where(imag, pltpu.roll(x, 2, 1), -pltpu.roll(x, 6, 1))
        x, turned = (v.astype(BF16).reshape(-1, CHANNELS) for v in (x, turned))
        cross = dot_tn(x, jnp.concatenate([x, turned], axis=1))
        parts.append([cross[:, :CHANNELS], cross[:, CHANNELS:]])
    row = lax.broadcasted_iota(jnp.int32, (CHANNELS, CHANNELS), 0)
    lane = lax.broadcasted_iota(jnp.int32, (CHANNELS, CHANNELS), 1)
    for down, right in ((4, 32), (2, 16), (1, 8)):
        row_bit = (row & down) != 0
        lane_bit = (lane & right) != 0
        for f in range(2):
            for part in range(2):
                a = parts[f][part]
                up = pltpu.roll(pltpu.roll(a, CHANNELS - down, 0), right, 1)
                dn = pltpu.roll(pltpu.roll(a, down, 0), CHANNELS - right, 1)
                parts[f][part] = jnp.where(row_bit == lane_bit, a, jnp.where(row_bit, dn, up))
    lane_bit = (lane & 64) != 0
    for part in range(2):
        for high, a in enumerate(swap_halves(parts[0][part], parts[1][part], lane_bit, 64, 1)):
            for c in range(CHANNELS // 8):
                start = c * 32 + high * 16 + part
                out_ref[pl.ds(start, 8, stride=2), :] = a[c * 8 : c * 8 + 8]


def lag_kernel(c_ref, hi_ref, lo_ref, out_ref):
    turned = c_ref[...].T
    hi, lo = two_terms(jnp.concatenate([turned[:64], turned[64:]], axis=1))
    both = dot_nn(jnp.concatenate([hi, lo], axis=0), hi_ref[...])
    total = both[:64] + (both[64:] + dot_nn(hi, lo_ref[...]))
    out_ref[...] = total.astype(BF16)


def kernel_call(kernel, out_shape, name, args, in_hbm=(), scratch=(), limit=24):
    vmem, hbm = pl.BlockSpec(memory_space=pltpu.VMEM), pl.BlockSpec(memory_space=pl.ANY)
    return pl.pallas_call(
        kernel,
        in_specs=[hbm if k in in_hbm else vmem for k in range(len(args))],
        out_specs=vmem,
        out_shape=out_shape,
        scratch_shapes=scratch,
        name=name,
        compiler_params=pltpu.CompilerParams(vmem_limit_bytes=limit << 20),
    )(*[pltpu.with_memory_space_constraint(a, pltpu.HBM if k in in_hbm else pltpu.VMEM) for k, a in enumerate(args)])


def body(records, fir_taps):
    forward, near, (inv_hi, inv_lo), taps_table = tables()
    y = lax.all_to_all(records, "chan", 0, 0, tiled=True)
    y = y.reshape(LENGTH // CHANNELS, 2 * CHANNELS, CHANNELS)
    response = jnp.dot(
        taps_table,
        jnp.broadcast_to(fir_taps[:, None], (TAPS, 128)),
        precision=lax.Precision.HIGHEST,
        preferred_element_type=F32,
    )
    even, half, odd = forward
    staged = (even, half, near, response)
    white = kernel_call(
        whiten_kernel,
        pltpu.VMEM((2, PER_CLASS // 8, 8, 8, CHANNELS), BF16),
        "whiten",
        (y, odd, *staged),
        in_hbm=(2, 3, 4, 5),
        scratch=[*(pltpu.VMEM(t.shape, t.dtype) for t in staged), pltpu.SemaphoreType.DMA((len(staged),))],
    )
    owners = BAND // 2
    white = lax.all_to_all(white.reshape(owners, 8, CHANNELS), BOTH, 0, 0, tiled=True)
    cross = kernel_call(
        cross_kernel,
        pltpu.VMEM((2 * owners, 128), F32),
        "cross",
        (white.reshape(owners // 2, 16, CHANNELS),),
    )
    cross = lax.all_to_all(cross.reshape(owners, 2, 128), BOTH, 0, 0, tiled=True)
    lagged = kernel_call(
        lag_kernel,
        jax.ShapeDtypeStruct((64, 2 * LAGS), BF16),
        "lag",
        (cross.reshape(2 * owners, 128), inv_hi, inv_lo),
    )
    return lagged.reshape(8, 8, 2 * LAGS)


def solution(mesh):
    in_specs = (P("win", None, "chan"), P())
    out_specs = P("chan", "win", None)
    return jax.shard_map(body, mesh=mesh, in_specs=in_specs, out_specs=out_specs, check_vma=False)
```

```python
import functools
import math

import jax
import jax.numpy as jnp
import ml_dtypes
import numpy as np
from jax import lax
from jax.experimental import pallas as pl
from jax.experimental.pallas import tpu as pltpu
from jax.sharding import PartitionSpec as P

LENGTH = 2048
BAND = 512
FIRST_BIN = 16
LAGS = 512
HALF_WIDTH = 32
TAPS = 64
CHANNELS = 128
WINDOWS = 512
BOTH = ("chan", "win")
RADIX = 4
QUARTER = LENGTH // RADIX
PER_CLASS = BAND // RADIX

BF16 = jnp.bfloat16
F32 = jnp.float32


def split_table(table):
    hi = table.astype(ml_dtypes.bfloat16)
    lo = (table - hi.astype(np.float64)).astype(ml_dtypes.bfloat16)
    return hi, lo


def phases(rows, cols):
    return 2.0 * math.pi / LENGTH * np.mod(rows[:, None] * cols[None, :], LENGTH).astype(np.float64)


@functools.cache
def tables():
    order = (RADIX * np.arange(PER_CLASS)[None, :] + np.arange(RADIX)[:, None]).reshape(-1)
    bins = FIRST_BIN + order
    cos, sin = (f(phases(bins, np.arange(QUARTER))).reshape(RADIX, PER_CLASS, QUARTER) for f in (np.cos, np.sin))
    even = [np.concatenate([cos[r], -sin[r]]) for r in (0, 2)]
    odd = np.concatenate(
        [
            np.concatenate([np.concatenate([cos[r], -s * sin[r]], axis=1), np.concatenate([-sin[r], -s * cos[r]], axis=1)])
            for r, s in ((1, 1), (3, -1))
        ]
    )
    forward = [np.concatenate(split_table(t)) for t in (*even, odd)]
    offset = np.mod(order[:, None] - order[None, :], BAND)
    near = (offset <= HALF_WIDTH) | (offset >= BAND - HALF_WIDTH)
    angles = phases(bins, np.arange(TAPS))
    taps = np.concatenate([np.cos(angles), -np.sin(angles)]).astype(np.float32)
    owned = order.reshape(2, 2, PER_CLASS).transpose(1, 2, 0).reshape(-1)
    angles = phases(FIRST_BIN + owned, np.arange(2 * LAGS) - LAGS)
    inverse = np.stack([np.cos(angles), -np.sin(angles)], axis=1) / (WINDOWS * BAND)
    return forward, near.astype(ml_dtypes.bfloat16), np.concatenate(split_table(inverse.reshape(2 * BAND, 2 * LAGS))), taps


def dot_nt(a, b):
    return lax.dot_general(a, b, (((1,), (1,)), ((), ())), preferred_element_type=F32)


def dot_tn(a, b):
    return lax.dot_general(a, b, (((0,), (0,)), ((), ())), preferred_element_type=F32)


def dot_nn(a, b):
    return jnp.dot(a, b, preferred_element_type=F32)


def two_terms(x):
    hi = x.astype(BF16)
    return hi, (x - hi.astype(F32)).astype(BF16)


def swap_halves(low, high, bit, shift, axis):
    size = low.shape[axis]
    new_low = jnp.where(bit, pltpu.roll(high, shift, axis), low)
    new_high = jnp.where(bit, high, pltpu.roll(low, size - shift, axis))
    return new_low, new_high


def whiten_kernel(
    y_ref, odd_ref, even_hbm, half_hbm, near_hbm, resp_hbm, out_ref, even_ref, half_ref, near_ref, resp_ref, sems
):
    pairs = ((even_hbm, even_ref), (half_hbm, half_ref), (resp_hbm, resp_ref), (near_hbm, near_ref))
    copies = [pltpu.make_async_copy(src, dst, sems.at[k]) for k, (src, dst) in enumerate(pairs)]
    for copy in copies:
        copy.start()
    blocks = y_ref.shape[0] // RADIX
    sums = [[], [], [], []]
    for j in range(blocks):
        u = [y_ref[h * blocks + j].astype(F32) for h in range(RADIX)]
        even, odd = u[0] + u[2], u[1] + u[3]
        for k, x in enumerate((even + odd, even - odd, u[0] - u[2], u[1] - u[3])):
            sums[k].append(two_terms(x))
    terms = [[jnp.concatenate([x[t] for x in s], axis=1) for t in range(2)] for s in sums]
    inputs = [terms[0], terms[1], [jnp.concatenate([terms[2][t], terms[3][t]], axis=1) for t in range(2)]]
    spec = []
    for k, ref in enumerate((even_ref, half_ref, odd_ref)):
        hi, lo = inputs[k]
        rows = ref.shape[0] // 2
        if k < 2:
            copies[k].wait()
        both = dot_nt(ref[...], hi)
        spec.append(both[:rows] + both[rows:] + dot_nt(ref[:rows], lo))
    copies[2].wait()
    copies[3].wait()
    m = PER_CLASS
    spec_re = jnp.concatenate([spec[0][:m], spec[2][:m], spec[1][:m], spec[2][2 * m : 3 * m]])
    spec_im = jnp.concatenate([spec[0][m:], spec[2][m : 2 * m], spec[1][m:], spec[2][3 * m :]])
    resp_re = jnp.concatenate([resp_ref[:BAND]] * 2, axis=1)
    resp_im = jnp.concatenate([resp_ref[BAND:]] * 2, axis=1)
    filt_re = spec_re * resp_re - spec_im * resp_im
    filt_im = spec_re * resp_im + spec_im * resp_re
    power = filt_re * filt_re + filt_im * filt_im
    first = power.astype(BF16)
    second, third = two_terms(power - first.astype(F32))
    near = near_ref[...]
    smooth = (dot_nn(near, first) + dot_nn(near, second) + dot_nn(near, third)) * (1.0 / (2 * HALF_WIDTH + 1))
    inv_amp = lax.rsqrt(smooth + 1e-06)
    white = (filt_re * inv_amp, filt_im * inv_amp)
    row = lax.broadcasted_iota(jnp.int32, (m, CHANNELS), 0)
    bits = [(row & s) != 0 for s in (4, 2, 1)]
    for high in range(2):
        a = []
        for k in range(8):
            r = 2 * high + k // 4
            w = k % 2
            a.append(white[k // 2 % 2][r * m : (r + 1) * m, w * CHANNELS : (w + 1) * CHANNELS])
        for bit, shift in zip(bits, (4, 2, 1)):
            for k in range(8):
                if not k & shift:
                    a[k], a[k | shift] = swap_halves(a[k], a[k | shift], bit, shift, 0)
        for k in range(8):
            out_ref[:, k, high] = a[k].reshape(m // 8, 8, CHANNELS).astype(BF16)


def cross_kernel(core_ref, own_ref, other_ref, out_ref):
    core = core_ref[0]
    row = lax.broadcasted_iota(jnp.int32, (CHANNELS, CHANNELS), 0)
    lane = lax.broadcasted_iota(jnp.int32, (CHANNELS, CHANNELS), 1)
    odd_block = (lane & 8) != 0
    for high in range(2):
        own, other = (ref[:, high * 8 : high * 8 + 8].astype(F32) for ref in (own_ref, other_ref))
        bit = (lax.broadcasted_iota(jnp.int32, own.shape, 1) & 4) != 0
        imag = (lax.broadcasted_iota(jnp.int32, own.shape, 1) & 2) != 0
        parts = []
        for x in swap_halves(own, other, bit, 4, 1):
            turned = jnp.where(imag, pltpu.roll(x, 2, 1), -pltpu.roll(x, 6, 1))
            x, turned = (v.astype(BF16).reshape(-1, CHANNELS) for v in (x, turned))
            cross = dot_tn(x, jnp.concatenate([x, turned], axis=1))
            parts.append([cross[:, :CHANNELS], cross[:, CHANNELS:]])
        for part in range(2):
            even, odd = swap_halves(parts[0][part], parts[1][part], odd_block, 8, 1)
            a = jnp.where(core == 0, even, odd)
            for down, right in ((4, 64), (2, 32), (1, 16)):
                row_bit = (row & down) != 0
                lane_bit = (lane & right) != 0
                up = pltpu.roll(pltpu.roll(a, CHANNELS - down, 0), right, 1)
                dn = pltpu.roll(pltpu.roll(a, down, 0), CHANNELS - right, 1)
                a = jnp.where(row_bit == lane_bit, a, jnp.where(row_bit, dn, up))
            out_ref[pl.ds(2 * high + part, CHANNELS, stride=4), :] = a


def lag_kernel(c_ref, table_ref, out_ref):
    turned = c_ref[...].T.reshape(8, 2, 8, 4 * CHANNELS)
    hi, lo = two_terms(jnp.concatenate([turned[:, f].reshape(64, 4 * CHANNELS) for f in range(2)], axis=1))
    both = dot_nn(jnp.concatenate([hi, lo], axis=0), table_ref[: 2 * BAND])
    total = both[:64] + (both[64:] + dot_nn(hi, table_ref[2 * BAND :]))
    out_ref[...] = total.astype(BF16)


def kernel_call(kernel, out_shape, name, args, in_hbm=(), in_smem=(), scratch=(), cost=None, limit=24):
    specs, operands = [], []
    for k, a in enumerate(args):
        if k in in_smem:
            specs.append(pl.BlockSpec(memory_space=pltpu.SMEM))
        elif k in in_hbm:
            specs.append(pl.BlockSpec(memory_space=pl.ANY))
            a = pltpu.with_memory_space_constraint(a, pltpu.HBM)
        else:
            specs.append(pl.BlockSpec(memory_space=pltpu.VMEM))
            a = pltpu.with_memory_space_constraint(a, pltpu.VMEM)
        operands.append(a)
    return pl.pallas_call(
        kernel,
        in_specs=specs,
        out_specs=pl.BlockSpec(memory_space=pltpu.VMEM),
        out_shape=out_shape,
        scratch_shapes=scratch,
        name=name,
        cost_estimate=cost,
        compiler_params=pltpu.CompilerParams(vmem_limit_bytes=limit << 20),
    )(*operands)


def body(records, fir_taps):
    forward, near, inverse, taps_table = tables()
    y = lax.all_to_all(records, "chan", 0, 0, tiled=True)
    y = y.reshape(LENGTH // CHANNELS, 2 * CHANNELS, CHANNELS)
    response = jnp.dot(
        taps_table,
        jnp.broadcast_to(fir_taps[:, None], (TAPS, 128)),
        precision=lax.Precision.HIGHEST,
        preferred_element_type=F32,
    )
    even, half, odd = forward
    staged = (even, half, near, response)
    white = kernel_call(
        whiten_kernel,
        pltpu.VMEM((PER_CLASS // 8, 8, 2, 8, CHANNELS), BF16),
        "whiten",
        (y, odd, *staged),
        in_hbm=(2, 3, 4, 5),
        scratch=[*(pltpu.VMEM(t.shape, t.dtype) for t in staged), pltpu.SemaphoreType.DMA((len(staged),))],
    )
    owners = PER_CLASS
    groups = [list(range(core, 2 * owners, 2)) for core in range(2)]
    white = white.reshape(owners, 16, CHANNELS)
    white = lax.all_to_all(white, BOTH, 0, 0, tiled=True, axis_index_groups=groups)
    other = lax.ppermute(white, BOTH, [(d, d ^ 1) for d in range(2 * owners)])
    core = lax.rem(lax.axis_index("win"), 2).astype(jnp.int32).reshape(1)
    cross = kernel_call(
        cross_kernel,
        pltpu.VMEM((4 * owners, 128), F32),
        "cross",
        (core, white, other),
        in_smem=(0,),
        cost=pl.CostEstimate(flops=2 * 10**9, transcendentals=0, bytes_accessed=4 * 10**6),
    )
    cross = lax.all_to_all(cross.reshape(owners, 4, 128), BOTH, 0, 0, tiled=True, axis_index_groups=groups)
    lagged = kernel_call(
        lag_kernel,
        jax.ShapeDtypeStruct((64, 2 * LAGS), BF16),
        "lag",
        (cross.reshape(4 * owners, 128), inverse),
    )
    return lagged.reshape(8, 8, 2 * LAGS)


def solution(mesh):
    in_specs = (P("win", None, "chan"), P())
    out_specs = P("chan", "win", None)
    return jax.shard_map(body, mesh=mesh, in_specs=in_specs, out_specs=out_specs, check_vma=False)
```

```python
import functools
import math

import jax
import jax.numpy as jnp
import ml_dtypes
import numpy as np
from jax import lax
from jax.experimental import pallas as pl
from jax.experimental.pallas import tpu as pltpu
from jax.sharding import PartitionSpec as P

LENGTH = 2048
BAND = 512
FIRST_BIN = 16
LAGS = 512
HALF_WIDTH = 32
TAPS = 64
CHANNELS = 128
WINDOWS = 512
BOTH = ("win", "chan")
RADIX = 4
QUARTER = LENGTH // RADIX
PER_CLASS = BAND // RADIX

BF16 = jnp.bfloat16
F32 = jnp.float32


def split_table(table):
    hi = table.astype(ml_dtypes.bfloat16)
    lo = (table - hi.astype(np.float64)).astype(ml_dtypes.bfloat16)
    return hi, lo


def phases(rows, cols):
    return 2.0 * math.pi / LENGTH * np.mod(rows[:, None] * cols[None, :], LENGTH).astype(np.float64)


@functools.cache
def tables():
    order = (RADIX * np.arange(PER_CLASS)[None, :] + np.arange(RADIX)[:, None]).reshape(-1)
    bins = FIRST_BIN + order
    cos, sin = (f(phases(bins, np.arange(QUARTER))).reshape(RADIX, PER_CLASS, QUARTER) for f in (np.cos, np.sin))
    even = [np.concatenate([cos[r], -sin[r]]) for r in (0, 2)]
    odd = np.concatenate(
        [
            np.concatenate([np.concatenate([cos[r], -s * sin[r]], axis=1), np.concatenate([-sin[r], -s * cos[r]], axis=1)])
            for r, s in ((1, 1), (3, -1))
        ]
    )
    forward = [np.concatenate(split_table(t)) for t in (*even, odd)]
    offset = np.mod(order[:, None] - order[None, :], BAND)
    near = (offset <= HALF_WIDTH) | (offset >= BAND - HALF_WIDTH)
    angles = phases(bins, np.arange(TAPS))
    taps = np.concatenate([np.cos(angles), -np.sin(angles)]).astype(np.float32)
    owned = order.reshape(2, 2, PER_CLASS).transpose(1, 0, 2).reshape(-1)
    angles = phases(FIRST_BIN + owned, np.arange(2 * LAGS) - LAGS)
    inverse = np.stack([np.cos(angles), -np.sin(angles)], axis=1) / (WINDOWS * BAND)
    return forward, near.astype(ml_dtypes.bfloat16), split_table(inverse.reshape(2 * BAND, 2 * LAGS)), taps


def dot_nt(a, b):
    return lax.dot_general(a, b, (((1,), (1,)), ((), ())), preferred_element_type=F32)


def dot_tn(a, b):
    return lax.dot_general(a, b, (((0,), (0,)), ((), ())), preferred_element_type=F32)


def dot_nn(a, b):
    return jnp.dot(a, b, preferred_element_type=F32)


def two_terms(x):
    hi = x.astype(BF16)
    return hi, (x - hi.astype(F32)).astype(BF16)


def swap_halves(low, high, bit, shift, axis):
    size = low.shape[axis]
    new_low = jnp.where(bit, pltpu.roll(high, shift, axis), low)
    new_high = jnp.where(bit, high, pltpu.roll(low, size - shift, axis))
    return new_low, new_high


def whiten_kernel(
    y_ref, odd_ref, even_hbm, half_hbm, near_hbm, resp_hbm, out_ref, even_ref, half_ref, near_ref, resp_ref, sems
):
    pairs = ((even_hbm, even_ref), (half_hbm, half_ref), (resp_hbm, resp_ref), (near_hbm, near_ref))
    copies = [pltpu.make_async_copy(src, dst, sems.at[k]) for k, (src, dst) in enumerate(pairs)]
    for copy in copies:
        copy.start()
    blocks = y_ref.shape[0] // RADIX
    sums = [[], [], [], []]
    for j in range(blocks):
        u = [y_ref[h * blocks + j].astype(F32) for h in range(RADIX)]
        even, odd = u[0] + u[2], u[1] + u[3]
        for k, x in enumerate((even + odd, even - odd, u[0] - u[2], u[1] - u[3])):
            sums[k].append(two_terms(x))
    terms = [[jnp.concatenate([x[t] for x in s], axis=1) for t in range(2)] for s in sums]
    inputs = [terms[0], terms[1], [jnp.concatenate([terms[2][t], terms[3][t]], axis=1) for t in range(2)]]
    spec = {}
    for k, ref in ((2, odd_ref), (0, even_ref), (1, half_ref)):
        hi, lo = inputs[k]
        rows = ref.shape[0] // 2
        if k < 2:
            copies[k].wait()
        both = dot_nt(ref[...], hi)
        spec[k] = both[:rows] + both[rows:] + dot_nt(ref[:rows], lo)
    copies[2].wait()
    copies[3].wait()
    m = PER_CLASS
    spec_re = jnp.concatenate([spec[0][:m], spec[2][:m], spec[1][:m], spec[2][2 * m : 3 * m]])
    spec_im = jnp.concatenate([spec[0][m:], spec[2][m : 2 * m], spec[1][m:], spec[2][3 * m :]])
    resp_re = jnp.concatenate([resp_ref[:BAND]] * 2, axis=1)
    resp_im = jnp.concatenate([resp_ref[BAND:]] * 2, axis=1)
    filt_re = spec_re * resp_re - spec_im * resp_im
    filt_im = spec_re * resp_im + spec_im * resp_re
    power = filt_re * filt_re + filt_im * filt_im
    hi, lo = two_terms(power)
    near = near_ref[...]
    smooth = (dot_nn(near, hi) + dot_nn(near, lo)) * (1.0 / (2 * HALF_WIDTH + 1))
    inv_amp = lax.rsqrt(smooth + 1e-06)
    white = (filt_re * inv_amp, filt_im * inv_amp)
    row = lax.broadcasted_iota(jnp.int32, (m, CHANNELS), 0)
    bits = [(row & s) != 0 for s in (4, 2, 1)]
    for high in range(2):
        a = []
        for k in range(8):
            r = 2 * high + k // 4
            w = k % 2
            a.append(white[k // 2 % 2][r * m : (r + 1) * m, w * CHANNELS : (w + 1) * CHANNELS])
        for bit, shift in zip(bits, (4, 2, 1)):
            for k in range(8):
                if not k & shift:
                    a[k], a[k | shift] = swap_halves(a[k], a[k | shift], bit, shift, 0)
        for k in range(8):
            out_ref[high, :, k] = a[k].reshape(m // 8, 8, CHANNELS).astype(BF16)


def cross_kernel(b_ref, out_ref):
    wide = b_ref[...].astype(F32)
    first, second = wide[:, :8], wide[:, 8:]
    bit = (lax.broadcasted_iota(jnp.int32, first.shape, 1) & 4) != 0
    imag = (lax.broadcasted_iota(jnp.int32, first.shape, 1) & 2) != 0
    parts = []
    for x in swap_halves(first, second, bit, 4, 1):
        turned = jnp.where(imag, pltpu.roll(x, 2, 1), -pltpu.roll(x, 6, 1))
        x, turned = (v.astype(BF16).reshape(-1, CHANNELS) for v in (x, turned))
        cross = dot_tn(x, jnp.concatenate([x, turned], axis=1))
        parts.append([cross[:, :CHANNELS], cross[:, CHANNELS:]])
    row = lax.broadcasted_iota(jnp.int32, (CHANNELS, CHANNELS), 0)
    lane = lax.broadcasted_iota(jnp.int32, (CHANNELS, CHANNELS), 1)
    for down, right in ((4, 32), (2, 16), (1, 8)):
        row_bit = (row & down) != 0
        lane_bit = (lane & right) != 0
        for f in range(2):
            for part in range(2):
                a = parts[f][part]
                up = pltpu.roll(pltpu.roll(a, CHANNELS - down, 0), right, 1)
                dn = pltpu.roll(pltpu.roll(a, down, 0), CHANNELS - right, 1)
                parts[f][part] = jnp.where(row_bit == lane_bit, a, jnp.where(row_bit, dn, up))
    lane_bit = (lane & 64) != 0
    for part in range(2):
        for high, a in enumerate(swap_halves(parts[0][part], parts[1][part], lane_bit, 64, 1)):
            for c in range(CHANNELS // 8):
                start = high * 256 + c * 2 + part
                out_ref[pl.ds(start, 8, stride=32), :] = a[c * 8 : c * 8 + 8]


def lag_kernel(c_ref, hi_ref, lo_ref, out_ref):
    turned = c_ref[...].T
    hi, lo = two_terms(jnp.concatenate([turned[:64], turned[64:]], axis=1))
    both = dot_nn(jnp.concatenate([hi, lo], axis=0), hi_ref[...])
    total = both[:64] + (both[64:] + dot_nn(hi, lo_ref[...]))
    out_ref[...] = total.astype(BF16)


def kernel_call(kernel, out_shape, name, args, in_hbm=(), scratch=(), limit=24):
    vmem, hbm = pl.BlockSpec(memory_space=pltpu.VMEM), pl.BlockSpec(memory_space=pl.ANY)
    return pl.pallas_call(
        kernel,
        in_specs=[hbm if k in in_hbm else vmem for k in range(len(args))],
        out_specs=vmem,
        out_shape=out_shape,
        scratch_shapes=scratch,
        name=name,
        compiler_params=pltpu.CompilerParams(vmem_limit_bytes=limit << 20),
    )(*[pltpu.with_memory_space_constraint(a, pltpu.HBM if k in in_hbm else pltpu.VMEM) for k, a in enumerate(args)])


def body(records, fir_taps):
    forward, near, (inv_hi, inv_lo), taps_table = tables()
    y = lax.all_to_all(records, "chan", 0, 0, tiled=True)
    y = y.reshape(LENGTH // CHANNELS, 2 * CHANNELS, CHANNELS)
    response = jnp.dot(
        taps_table,
        jnp.broadcast_to(fir_taps[:, None], (TAPS, 128)),
        precision=lax.Precision.HIGHEST,
        preferred_element_type=F32,
    )
    even, half, odd = forward
    staged = (even, half, near, response)
    white = kernel_call(
        whiten_kernel,
        pltpu.VMEM((2, PER_CLASS // 8, 8, 8, CHANNELS), BF16),
        "whiten",
        (y, odd, *staged),
        in_hbm=(2, 3, 4, 5),
        scratch=[*(pltpu.VMEM(t.shape, t.dtype) for t in staged), pltpu.SemaphoreType.DMA((len(staged),))],
    )
    owners = BAND // 2
    white = lax.all_to_all(white.reshape(owners, 8, CHANNELS), BOTH, 0, 0, tiled=True)
    cross = kernel_call(
        cross_kernel,
        pltpu.VMEM((2 * owners, 128), F32),
        "cross",
        (white.reshape(owners // 2, 16, CHANNELS),),
    )
    cross = lax.all_to_all(cross.reshape(owners, 2, 128), BOTH, 0, 0, tiled=True)
    lagged = kernel_call(
        lag_kernel,
        jax.ShapeDtypeStruct((64, 2 * LAGS), BF16),
        "lag",
        (cross.reshape(2 * owners, 128), inv_hi, inv_lo),
    )
    return lagged.reshape(8, 8, 2 * LAGS)


def solution(mesh):
    in_specs = (P("win", None, "chan"), P())
    out_specs = P("chan", "win", None)
    return jax.shard_map(body, mesh=mesh, in_specs=in_specs, out_specs=out_specs, check_vma=False)
```

```python
import functools
import math

import jax
import jax.numpy as jnp
import ml_dtypes
import numpy as np
from jax import lax
from jax.experimental import pallas as pl
from jax.experimental.pallas import tpu as pltpu
from jax.sharding import PartitionSpec as P

LENGTH = 2048
BAND = 512
FIRST_BIN = 16
LAGS = 512
HALF_WIDTH = 32
TAPS = 64
CHANNELS = 128
WINDOWS = 512
BOTH = ("win", "chan")
RADIX = 4
QUARTER = LENGTH // RADIX
PER_CLASS = BAND // RADIX

BF16 = jnp.bfloat16
F32 = jnp.float32


def split_table(table):
    hi = table.astype(ml_dtypes.bfloat16)
    lo = (table - hi.astype(np.float64)).astype(ml_dtypes.bfloat16)
    return hi, lo


def phases(rows, cols):
    return 2.0 * math.pi / LENGTH * np.mod(rows[:, None] * cols[None, :], LENGTH).astype(np.float64)


@functools.cache
def tables():
    order = (RADIX * np.arange(PER_CLASS)[None, :] + np.arange(RADIX)[:, None]).reshape(-1)
    bins = FIRST_BIN + order
    cos, sin = (f(phases(bins, np.arange(QUARTER))).reshape(RADIX, PER_CLASS, QUARTER) for f in (np.cos, np.sin))
    even = [np.concatenate([cos[r], -sin[r]]) for r in (0, 2)]
    odd = np.concatenate(
        [
            np.concatenate([np.concatenate([cos[r], -s * sin[r]], axis=1), np.concatenate([-sin[r], -s * cos[r]], axis=1)])
            for r, s in ((1, 1), (3, -1))
        ]
    )
    forward = [np.concatenate(split_table(t)) for t in (*even, odd)]
    offset = np.mod(order[:, None] - order[None, :], BAND)
    near = (offset <= HALF_WIDTH) | (offset >= BAND - HALF_WIDTH)
    angles = phases(bins, np.arange(TAPS))
    taps = np.concatenate([np.cos(angles), -np.sin(angles)]).astype(np.float32)
    owned = order.reshape(2, 2, PER_CLASS).transpose(1, 0, 2).reshape(-1)
    angles = phases(FIRST_BIN + owned, np.arange(2 * LAGS) - LAGS)
    inverse = np.stack([np.cos(angles), -np.sin(angles)], axis=1) / (WINDOWS * BAND)
    return forward, near.astype(ml_dtypes.bfloat16), split_table(inverse.reshape(2 * BAND, 2 * LAGS)), taps


def dot_nt(a, b):
    return lax.dot_general(a, b, (((1,), (1,)), ((), ())), preferred_element_type=F32)


def dot_tn(a, b):
    return lax.dot_general(a, b, (((0,), (0,)), ((), ())), preferred_element_type=F32)


def dot_nn(a, b):
    return jnp.dot(a, b, preferred_element_type=F32)


def two_terms(x):
    hi = x.astype(BF16)
    return hi, (x - hi.astype(F32)).astype(BF16)


def swap_halves(low, high, bit, shift, axis):
    size = low.shape[axis]
    new_low = jnp.where(bit, pltpu.roll(high, shift, axis), low)
    new_high = jnp.where(bit, high, pltpu.roll(low, size - shift, axis))
    return new_low, new_high


def whiten_kernel(
    y_ref, even_ref, half_ref, near_ref, resp_ref, odd_hbm, out_ref, odd_ref, sem
):
    copy = pltpu.make_async_copy(odd_hbm, odd_ref, sem)
    copy.start()
    blocks = y_ref.shape[0] // RADIX
    sums = [[], [], [], []]
    for j in range(blocks):
        u = [y_ref[h * blocks + j].astype(F32) for h in range(RADIX)]
        even, odd = u[0] + u[2], u[1] + u[3]
        for k, x in enumerate((even + odd, even - odd, u[0] - u[2], u[1] - u[3])):
            sums[k].append(two_terms(x))
    terms = [[jnp.concatenate([x[t] for x in s], axis=1) for t in range(2)] for s in sums]
    inputs = [terms[0], terms[1], [jnp.concatenate([terms[2][t], terms[3][t]], axis=1) for t in range(2)]]
    spec = [None] * 3
    for k, ref in enumerate((even_ref, half_ref, odd_ref)):
        hi, lo = inputs[k]
        rows = ref.shape[0] // 2
        if k == 2:
            copy.wait()
        both = dot_nt(ref[...], hi)
        spec[k] = both[:rows] + both[rows:] + dot_nt(ref[:rows], lo)
    m = PER_CLASS
    spec_re = jnp.concatenate([spec[0][:m], spec[2][:m], spec[1][:m], spec[2][2 * m : 3 * m]])
    spec_im = jnp.concatenate([spec[0][m:], spec[2][m : 2 * m], spec[1][m:], spec[2][3 * m :]])
    resp_re = jnp.concatenate([resp_ref[:BAND]] * 2, axis=1)
    resp_im = jnp.concatenate([resp_ref[BAND:]] * 2, axis=1)
    filt_re = spec_re * resp_re - spec_im * resp_im
    filt_im = spec_re * resp_im + spec_im * resp_re
    power = filt_re * filt_re + filt_im * filt_im
    hi, lo = two_terms(power)
    near = near_ref[...]
    smooth = (dot_nn(near, hi) + dot_nn(near, lo)) * (1.0 / (2 * HALF_WIDTH + 1))
    inv_amp = lax.rsqrt(smooth + 1e-06)
    white = (filt_re * inv_amp, filt_im * inv_amp)
    row = lax.broadcasted_iota(jnp.int32, (m, CHANNELS), 0)
    bits = [(row & s) != 0 for s in (4, 2, 1)]
    for high in range(2):
        a = []
        for k in range(8):
            r = 2 * high + k // 4
            w = k % 2
            a.append(white[k // 2 % 2][r * m : (r + 1) * m, w * CHANNELS : (w + 1) * CHANNELS])
        for bit, shift in zip(bits, (4, 2, 1)):
            for k in range(8):
                if not k & shift:
                    a[k], a[k | shift] = swap_halves(a[k], a[k | shift], bit, shift, 0)
        for k in range(8):
            out_ref[high, :, k] = a[k].reshape(m // 8, 8, CHANNELS).astype(BF16)


def cross_kernel(b_ref, out_ref):
    wide = b_ref[...].astype(F32)
    first, second = wide[:, :8], wide[:, 8:]
    bit = (lax.broadcasted_iota(jnp.int32, first.shape, 1) & 4) != 0
    imag = (lax.broadcasted_iota(jnp.int32, first.shape, 1) & 2) != 0
    parts = []
    for x in swap_halves(first, second, bit, 4, 1):
        turned = jnp.where(imag, pltpu.roll(x, 2, 1), -pltpu.roll(x, 6, 1))
        x, turned = (v.astype(BF16).reshape(-1, CHANNELS) for v in (x, turned))
        cross = dot_tn(x, jnp.concatenate([x, turned], axis=1))
        parts.append([cross[:, :CHANNELS], cross[:, CHANNELS:]])
    row = lax.broadcasted_iota(jnp.int32, (CHANNELS, CHANNELS), 0)
    lane = lax.broadcasted_iota(jnp.int32, (CHANNELS, CHANNELS), 1)
    for down, right in ((4, 32), (2, 16), (1, 8)):
        row_bit = (row & down) != 0
        lane_bit = (lane & right) != 0
        for f in range(2):
            for part in range(2):
                a = parts[f][part]
                up = pltpu.roll(pltpu.roll(a, CHANNELS - down, 0), right, 1)
                dn = pltpu.roll(pltpu.roll(a, down, 0), CHANNELS - right, 1)
                parts[f][part] = jnp.where(row_bit == lane_bit, a, jnp.where(row_bit, dn, up))
    lane_bit = (lane & 64) != 0
    for part in range(2):
        for high, a in enumerate(swap_halves(parts[0][part], parts[1][part], lane_bit, 64, 1)):
            for c in range(CHANNELS // 8):
                start = high * 256 + c * 2 + part
                out_ref[pl.ds(start, 8, stride=32), :] = a[c * 8 : c * 8 + 8]


def lag_kernel(c_ref, hi_ref, lo_ref, out_ref):
    turned = c_ref[...].T
    hi, lo = two_terms(jnp.concatenate([turned[:64], turned[64:]], axis=1))
    both = dot_nn(jnp.concatenate([hi, lo], axis=0), hi_ref[...])
    total = both[:64] + (both[64:] + dot_nn(hi, lo_ref[...]))
    out_ref[...] = total.astype(BF16)


def kernel_call(kernel, out_shape, name, args, in_hbm=(), scratch=(), cost=None, limit=24):
    vmem, hbm = pl.BlockSpec(memory_space=pltpu.VMEM), pl.BlockSpec(memory_space=pl.ANY)
    return pl.pallas_call(
        kernel,
        in_specs=[hbm if k in in_hbm else vmem for k in range(len(args))],
        out_specs=vmem,
        out_shape=out_shape,
        scratch_shapes=scratch,
        name=name,
        cost_estimate=cost,
        compiler_params=pltpu.CompilerParams(vmem_limit_bytes=limit << 20),
    )(*[pltpu.with_memory_space_constraint(a, pltpu.HBM if k in in_hbm else pltpu.VMEM) for k, a in enumerate(args)])


def body(records, fir_taps):
    forward, near, (inv_hi, inv_lo), taps_table = tables()
    y = lax.all_to_all(records, "chan", 0, 0, tiled=True)
    y = y.reshape(LENGTH // CHANNELS, 2 * CHANNELS, CHANNELS)
    response = jnp.dot(
        taps_table,
        jnp.broadcast_to(fir_taps[:, None], (TAPS, 128)),
        precision=lax.Precision.HIGHEST,
        preferred_element_type=F32,
    )
    even, half, odd = forward
    white = kernel_call(
        whiten_kernel,
        pltpu.VMEM((2, PER_CLASS // 8, 8, 8, CHANNELS), BF16),
        "whiten",
        (y, even, half, near, response, odd),
        in_hbm=(5,),
        scratch=[pltpu.VMEM(odd.shape, BF16), pltpu.SemaphoreType.DMA(())],
    )
    owners = BAND // 2
    white = lax.all_to_all(white.reshape(owners, 8, CHANNELS), BOTH, 0, 0, tiled=True)
    cross = kernel_call(
        cross_kernel,
        pltpu.VMEM((2 * owners, 128), F32),
        "cross",
        (white.reshape(owners // 2, 16, CHANNELS),),
        cost=pl.CostEstimate(flops=2 * 10**9, transcendentals=0, bytes_accessed=4 * 10**6),
    )
    cross = lax.all_to_all(cross.reshape(owners, 2, 128), BOTH, 0, 0, tiled=True)
    lagged = kernel_call(
        lag_kernel,
        jax.ShapeDtypeStruct((64, 2 * LAGS), BF16),
        "lag",
        (cross.reshape(2 * owners, 128), inv_hi, inv_lo),
    )
    return lagged.reshape(8, 8, 2 * LAGS)


def solution(mesh):
    in_specs = (P("win", None, "chan"), P())
    out_specs = P("chan", "win", None)
    return jax.shard_map(body, mesh=mesh, in_specs=in_specs, out_specs=out_specs, check_vma=False)
```

```python
import functools
import math

import jax
import jax.numpy as jnp
import ml_dtypes
import numpy as np
from jax import lax
from jax.experimental import pallas as pl
from jax.experimental.pallas import tpu as pltpu
from jax.sharding import PartitionSpec as P

LENGTH = 2048
BAND = 512
FIRST_BIN = 16
LAGS = 512
HALF_WIDTH = 32
TAPS = 64
CHANNELS = 128
WINDOWS = 512
BOTH = ("win", "chan")
RADIX = 4
QUARTER = LENGTH // RADIX
PER_CLASS = BAND // RADIX

ORDER = [2 * z + x for z in (0, 4, 1, 5, 2, 6, 3, 7) for x in (0, 1)]
BF16 = jnp.bfloat16
F32 = jnp.float32


def split_table(table):
    hi = table.astype(ml_dtypes.bfloat16)
    lo = (table - hi.astype(np.float64)).astype(ml_dtypes.bfloat16)
    return hi, lo


def phases(rows, cols):
    return 2.0 * math.pi / LENGTH * np.mod(rows[:, None] * cols[None, :], LENGTH).astype(np.float64)


@functools.cache
def tables():
    order = (RADIX * np.arange(PER_CLASS)[None, :] + np.arange(RADIX)[:, None]).reshape(-1)
    bins = FIRST_BIN + order
    cos, sin = (f(phases(bins, np.arange(QUARTER))).reshape(RADIX, PER_CLASS, QUARTER) for f in (np.cos, np.sin))
    even = [np.concatenate([cos[r], -sin[r]]) for r in (0, 2)]
    odd = np.concatenate(
        [
            np.concatenate([np.concatenate([cos[r], -s * sin[r]], axis=1), np.concatenate([-sin[r], -s * cos[r]], axis=1)])
            for r, s in ((1, 1), (3, -1))
        ]
    )
    forward = [np.concatenate(split_table(t)) for t in (*even, odd)]
    offset = np.mod(order[:, None] - order[None, :], BAND)
    near = (offset <= HALF_WIDTH) | (offset >= BAND - HALF_WIDTH)
    angles = phases(bins, np.arange(TAPS))
    taps = np.concatenate([np.cos(angles), -np.sin(angles)]).astype(np.float32)
    owned = order.reshape(2, 2, PER_CLASS).transpose(1, 0, 2).reshape(-1)
    angles = phases(FIRST_BIN + owned, np.arange(2 * LAGS) - LAGS)
    inverse = np.stack([np.cos(angles), -np.sin(angles)], axis=1) / (WINDOWS * BAND)
    return forward, near.astype(ml_dtypes.bfloat16), split_table(inverse.reshape(2 * BAND, 2 * LAGS)), taps


def dot_nt(a, b):
    return lax.dot_general(a, b, (((1,), (1,)), ((), ())), preferred_element_type=F32)


def dot_tn(a, b):
    return lax.dot_general(a, b, (((0,), (0,)), ((), ())), preferred_element_type=F32)


def dot_nn(a, b):
    return jnp.dot(a, b, preferred_element_type=F32)


def two_terms(x):
    hi = x.astype(BF16)
    return hi, (x - hi.astype(F32)).astype(BF16)


def swap_halves(low, high, bit, shift, axis):
    size = low.shape[axis]
    new_low = jnp.where(bit, pltpu.roll(high, shift, axis), low)
    new_high = jnp.where(bit, high, pltpu.roll(low, size - shift, axis))
    return new_low, new_high


def whiten_kernel(
    y_ref, even_ref, half_ref, near_ref, resp_ref, odd_hbm, out_ref, odd_ref, sem
):
    copy = pltpu.make_async_copy(odd_hbm, odd_ref, sem)
    copy.start()
    blocks = y_ref.shape[0] // RADIX
    sums = [[], [], [], []]
    for j in range(blocks):
        u = [y_ref[ORDER.index(h * blocks + j)].astype(F32) for h in range(RADIX)]
        even, odd = u[0] + u[2], u[1] + u[3]
        for k, x in enumerate((even + odd, even - odd, u[0] - u[2], u[1] - u[3])):
            sums[k].append(two_terms(x))
    terms = [[jnp.concatenate([x[t] for x in s], axis=1) for t in range(2)] for s in sums]
    inputs = [terms[0], terms[1], [jnp.concatenate([terms[2][t], terms[3][t]], axis=1) for t in range(2)]]
    spec = [None] * 3
    for k, ref in enumerate((even_ref, half_ref, odd_ref)):
        hi, lo = inputs[k]
        rows = ref.shape[0] // 2
        if k == 2:
            copy.wait()
        both = dot_nt(ref[...], hi)
        spec[k] = both[:rows] + both[rows:] + dot_nt(ref[:rows], lo)
    m = PER_CLASS
    spec_re = jnp.concatenate([spec[0][:m], spec[2][:m], spec[1][:m], spec[2][2 * m : 3 * m]])
    spec_im = jnp.concatenate([spec[0][m:], spec[2][m : 2 * m], spec[1][m:], spec[2][3 * m :]])
    resp_re = jnp.concatenate([resp_ref[:BAND]] * 2, axis=1)
    resp_im = jnp.concatenate([resp_ref[BAND:]] * 2, axis=1)
    filt_re = spec_re * resp_re - spec_im * resp_im
    filt_im = spec_re * resp_im + spec_im * resp_re
    power = filt_re * filt_re + filt_im * filt_im
    hi, lo = two_terms(power)
    near = near_ref[...]
    smooth = (dot_nn(near, hi) + dot_nn(near, lo)) * (1.0 / (2 * HALF_WIDTH + 1))
    inv_amp = lax.rsqrt(smooth + 1e-06)
    white = (filt_re * inv_amp, filt_im * inv_amp)
    row = lax.broadcasted_iota(jnp.int32, (m, CHANNELS), 0)
    bits = [(row & s) != 0 for s in (4, 2, 1)]
    for high in range(2):
        a = []
        for k in range(8):
            r = 2 * high + k // 4
            w = k % 2
            a.append(white[k // 2 % 2][r * m : (r + 1) * m, w * CHANNELS : (w + 1) * CHANNELS])
        for bit, shift in zip(bits, (4, 2, 1)):
            for k in range(8):
                if not k & shift:
                    a[k], a[k | shift] = swap_halves(a[k], a[k | shift], bit, shift, 0)
        for k in range(8):
            out_ref[high, :, k] = a[k].reshape(m // 8, 8, CHANNELS).astype(BF16)


def cross_kernel(b_ref, out_ref):
    wide = b_ref[...].astype(F32)
    first, second = wide[:, :8], wide[:, 8:]
    bit = (lax.broadcasted_iota(jnp.int32, first.shape, 1) & 4) != 0
    imag = (lax.broadcasted_iota(jnp.int32, first.shape, 1) & 2) != 0
    parts = []
    for x in swap_halves(first, second, bit, 4, 1):
        turned = jnp.where(imag, pltpu.roll(x, 2, 1), -pltpu.roll(x, 6, 1))
        x, turned = (v.astype(BF16).reshape(-1, CHANNELS) for v in (x, turned))
        cross = dot_tn(x, jnp.concatenate([x, turned], axis=1))
        parts.append([cross[:, :CHANNELS], cross[:, CHANNELS:]])
    row = lax.broadcasted_iota(jnp.int32, (CHANNELS, CHANNELS), 0)
    lane = lax.broadcasted_iota(jnp.int32, (CHANNELS, CHANNELS), 1)
    for down, right in ((4, 32), (2, 16), (1, 8)):
        row_bit = (row & down) != 0
        lane_bit = (lane & right) != 0
        for f in range(2):
            for part in range(2):
                a = parts[f][part]
                up = pltpu.roll(pltpu.roll(a, CHANNELS - down, 0), right, 1)
                dn = pltpu.roll(pltpu.roll(a, down, 0), CHANNELS - right, 1)
                parts[f][part] = jnp.where(row_bit == lane_bit, a, jnp.where(row_bit, dn, up))
    lane_bit = (lane & 64) != 0
    for part in range(2):
        for high, a in enumerate(swap_halves(parts[0][part], parts[1][part], lane_bit, 64, 1)):
            for c in range(CHANNELS // 8):
                start = high * 256 + c * 2 + part
                out_ref[pl.ds(start, 8, stride=32), :] = a[c * 8 : c * 8 + 8]


def lag_kernel(c_ref, hi_ref, lo_ref, out_ref):
    turned = c_ref[...].T
    hi, lo = two_terms(jnp.concatenate([turned[:64], turned[64:]], axis=1))
    both = dot_nn(jnp.concatenate([hi, lo], axis=0), hi_ref[...])
    total = both[:64] + (both[64:] + dot_nn(hi, lo_ref[...]))
    out_ref[...] = total.astype(BF16)


def kernel_call(kernel, out_shape, name, args, in_hbm=(), scratch=(), cost=None, limit=24):
    vmem, hbm = pl.BlockSpec(memory_space=pltpu.VMEM), pl.BlockSpec(memory_space=pl.ANY)
    return pl.pallas_call(
        kernel,
        in_specs=[hbm if k in in_hbm else vmem for k in range(len(args))],
        out_specs=vmem,
        out_shape=out_shape,
        scratch_shapes=scratch,
        name=name,
        cost_estimate=cost,
        compiler_params=pltpu.CompilerParams(vmem_limit_bytes=limit << 20),
    )(*[pltpu.with_memory_space_constraint(a, pltpu.HBM if k in in_hbm else pltpu.VMEM) for k, a in enumerate(args)])


def body(records, fir_taps):
    forward, near, (inv_hi, inv_lo), taps_table = tables()
    y = lax.all_to_all(records, "chan", 0, 0, tiled=True, axis_index_groups=[ORDER])
    y = y.reshape(LENGTH // CHANNELS, 2 * CHANNELS, CHANNELS)
    response = jnp.dot(
        taps_table,
        jnp.broadcast_to(fir_taps[:, None], (TAPS, 128)),
        precision=lax.Precision.HIGHEST,
        preferred_element_type=F32,
    )
    even, half, odd = forward
    white = kernel_call(
        whiten_kernel,
        pltpu.VMEM((2, PER_CLASS // 8, 8, 8, CHANNELS), BF16),
        "whiten",
        (y, even, half, near, response, odd),
        in_hbm=(5,),
        scratch=[pltpu.VMEM(odd.shape, BF16), pltpu.SemaphoreType.DMA(())],
    )
    owners = BAND // 2
    white = lax.all_to_all(white.reshape(owners, 8, CHANNELS), BOTH, 0, 0, tiled=True)
    cross = kernel_call(
        cross_kernel,
        pltpu.VMEM((2 * owners, 128), F32),
        "cross",
        (white.reshape(owners // 2, 16, CHANNELS),),
        cost=pl.CostEstimate(flops=2 * 10**9, transcendentals=0, bytes_accessed=4 * 10**6),
    )
    cross = lax.all_to_all(cross.reshape(owners, 2, 128), BOTH, 0, 0, tiled=True)
    lagged = kernel_call(
        lag_kernel,
        jax.ShapeDtypeStruct((64, 2 * LAGS), BF16),
        "lag",
        (cross.reshape(2 * owners, 128), inv_hi, inv_lo),
    )
    return lagged.reshape(8, 8, 2 * LAGS)


def solution(mesh):
    in_specs = (P("win", None, "chan"), P())
    out_specs = P("chan", "win", None)
    return jax.shard_map(body, mesh=mesh, in_specs=in_specs, out_specs=out_specs, check_vma=False)
```

```python
import functools
import math

import jax
import jax.numpy as jnp
import ml_dtypes
import numpy as np
from jax import lax
from jax.experimental import pallas as pl
from jax.experimental.pallas import tpu as pltpu
from jax.sharding import PartitionSpec as P

LENGTH = 2048
BAND = 512
FIRST_BIN = 16
LAGS = 512
HALF_WIDTH = 32
TAPS = 64
CHANNELS = 128
WINDOWS = 512
BOTH = ("win", "chan")
RADIX = 4
QUARTER = LENGTH // RADIX
PER_CLASS = BAND // RADIX

ORDER = [2 * z + x for z in (0, 4, 1, 5, 2, 6, 3, 7) for x in (0, 1)]
BF16 = jnp.bfloat16
F32 = jnp.float32


def split_table(table):
    hi = table.astype(ml_dtypes.bfloat16)
    lo = (table - hi.astype(np.float64)).astype(ml_dtypes.bfloat16)
    return hi, lo


def phases(rows, cols):
    return 2.0 * math.pi / LENGTH * np.mod(rows[:, None] * cols[None, :], LENGTH).astype(np.float64)


@functools.cache
def tables():
    order = (RADIX * np.arange(PER_CLASS)[None, :] + np.arange(RADIX)[:, None]).reshape(-1)
    bins = FIRST_BIN + order
    cos, sin = (f(phases(bins, np.arange(QUARTER))).reshape(RADIX, PER_CLASS, QUARTER) for f in (np.cos, np.sin))
    even = [np.concatenate([cos[r], -sin[r]]) for r in (0, 2)]
    odd = np.concatenate(
        [
            np.concatenate([np.concatenate([cos[r], -s * sin[r]], axis=1), np.concatenate([-sin[r], -s * cos[r]], axis=1)])
            for r, s in ((1, 1), (3, -1))
        ]
    )
    forward = [np.concatenate(split_table(t)) for t in (*even, odd)]
    offset = np.mod(order[:, None] - order[None, :], BAND)
    near = (offset <= HALF_WIDTH) | (offset >= BAND - HALF_WIDTH)
    angles = phases(bins, np.arange(TAPS))
    taps = np.concatenate([np.cos(angles), -np.sin(angles)]).astype(np.float32)
    owned = order.reshape(2, 2, PER_CLASS).transpose(1, 0, 2).reshape(-1)
    angles = phases(FIRST_BIN + owned, np.arange(LAGS))
    inverse = np.stack([np.cos(angles), -np.sin(angles)], axis=1) / (WINDOWS * BAND)
    return forward, near.astype(ml_dtypes.bfloat16), split_table(inverse.reshape(2 * BAND, LAGS)), taps


def dot_nt(a, b):
    return lax.dot_general(a, b, (((1,), (1,)), ((), ())), preferred_element_type=F32)


def dot_tn(a, b):
    return lax.dot_general(a, b, (((0,), (0,)), ((), ())), preferred_element_type=F32)


def dot_nn(a, b):
    return jnp.dot(a, b, preferred_element_type=F32)


def two_terms(x):
    hi = x.astype(BF16)
    return hi, (x - hi.astype(F32)).astype(BF16)


def swap_halves(low, high, bit, shift, axis):
    size = low.shape[axis]
    new_low = jnp.where(bit, pltpu.roll(high, shift, axis), low)
    new_high = jnp.where(bit, high, pltpu.roll(low, size - shift, axis))
    return new_low, new_high


def whiten_kernel(
    y_ref, even_ref, half_ref, near_ref, resp_ref, odd_hbm, out_ref, odd_ref, sem
):
    copy = pltpu.make_async_copy(odd_hbm, odd_ref, sem)
    copy.start()
    blocks = y_ref.shape[0] // RADIX
    sums = [[], [], [], []]
    for j in range(blocks):
        u = [y_ref[ORDER.index(h * blocks + j)].astype(F32) for h in range(RADIX)]
        even, odd = u[0] + u[2], u[1] + u[3]
        for k, x in enumerate((even + odd, even - odd, u[0] - u[2], u[1] - u[3])):
            sums[k].append(two_terms(x))
    terms = [[jnp.concatenate([x[t] for x in s], axis=1) for t in range(2)] for s in sums]
    inputs = [terms[0], terms[1], [jnp.concatenate([terms[2][t], terms[3][t]], axis=1) for t in range(2)]]
    spec = [None] * 3
    for k, ref in enumerate((even_ref, half_ref, odd_ref)):
        hi, lo = inputs[k]
        rows = ref.shape[0] // 2
        if k == 2:
            copy.wait()
        both = dot_nt(ref[...], hi)
        spec[k] = both[:rows] + both[rows:] + dot_nt(ref[:rows], lo)
    m = PER_CLASS
    spec_re = jnp.concatenate([spec[0][:m], spec[2][:m], spec[1][:m], spec[2][2 * m : 3 * m]])
    spec_im = jnp.concatenate([spec[0][m:], spec[2][m : 2 * m], spec[1][m:], spec[2][3 * m :]])
    resp_re = jnp.concatenate([resp_ref[:BAND]] * 2, axis=1)
    resp_im = jnp.concatenate([resp_ref[BAND:]] * 2, axis=1)
    filt_re = spec_re * resp_re - spec_im * resp_im
    filt_im = spec_re * resp_im + spec_im * resp_re
    power = filt_re * filt_re + filt_im * filt_im
    hi, lo = two_terms(power)
    near = near_ref[...]
    smooth = (dot_nn(near, hi) + dot_nn(near, lo)) * (1.0 / (2 * HALF_WIDTH + 1))
    inv_amp = lax.rsqrt(smooth + 1e-06)
    white = (filt_re * inv_amp, filt_im * inv_amp)
    row = lax.broadcasted_iota(jnp.int32, (m, CHANNELS), 0)
    bits = [(row & s) != 0 for s in (4, 2, 1)]
    for high in range(2):
        a = []
        for k in range(8):
            r = 2 * high + k // 4
            w = k % 2
            a.append(white[k // 2 % 2][r * m : (r + 1) * m, w * CHANNELS : (w + 1) * CHANNELS])
        for bit, shift in zip(bits, (4, 2, 1)):
            for k in range(8):
                if not k & shift:
                    a[k], a[k | shift] = swap_halves(a[k], a[k | shift], bit, shift, 0)
        for k in range(8):
            out_ref[high, :, k] = a[k].reshape(m // 8, 8, CHANNELS).astype(BF16)


def cross_kernel(b_ref, out_ref):
    wide = b_ref[...].astype(F32)
    first, second = wide[:, :8], wide[:, 8:]
    bit = (lax.broadcasted_iota(jnp.int32, first.shape, 1) & 4) != 0
    imag = (lax.broadcasted_iota(jnp.int32, first.shape, 1) & 2) != 0
    parts = []
    for x in swap_halves(first, second, bit, 4, 1):
        turned = jnp.where(imag, pltpu.roll(x, 2, 1), -pltpu.roll(x, 6, 1))
        x, turned = (v.astype(BF16).reshape(-1, CHANNELS) for v in (x, turned))
        cross = dot_tn(x, jnp.concatenate([x, turned], axis=1))
        parts.append([cross[:, :CHANNELS], cross[:, CHANNELS:]])
    row = lax.broadcasted_iota(jnp.int32, (CHANNELS, CHANNELS), 0)
    lane = lax.broadcasted_iota(jnp.int32, (CHANNELS, CHANNELS), 1)
    for down, right in ((4, 32), (2, 16), (1, 8)):
        row_bit = (row & down) != 0
        lane_bit = (lane & right) != 0
        for f in range(2):
            for part in range(2):
                a = parts[f][part]
                up = pltpu.roll(pltpu.roll(a, CHANNELS - down, 0), right, 1)
                dn = pltpu.roll(pltpu.roll(a, down, 0), CHANNELS - right, 1)
                parts[f][part] = jnp.where(row_bit == lane_bit, a, jnp.where(row_bit, dn, up))
    lane_bit = (lane & 64) != 0
    for part in range(2):
        for high, a in enumerate(swap_halves(parts[0][part], parts[1][part], lane_bit, 64, 1)):
            for c in range(CHANNELS // 8):
                start = high * 256 + c * 2 + part
                out_ref[pl.ds(start, 8, stride=32), :] = a[c * 8 : c * 8 + 8]


def lag_kernel(c_ref, hi_ref, lo_ref, out_ref):
    c = c_ref[...]
    rows = c.shape[0]
    row = lax.broadcasted_iota(jnp.int32, c.shape, 0)
    imag = (row & 1) != 0
    late = row >= rows // 2
    low_class = lax.broadcasted_iota(jnp.int32, c.shape, 1) >= c.shape[1] // 2
    swapped = jnp.where(imag, pltpu.roll(c, 1, 0), pltpu.roll(c, rows - 1, 0))
    turned = jnp.where(low_class, jnp.where(imag, -swapped, swapped), c)
    turned = jnp.where(late, -turned, turned)
    halves = []
    for x in (c.T, turned.T):
        halves.append(jnp.concatenate([x[:64], x[64:]], axis=1))
    hi, lo = two_terms(jnp.concatenate(halves, axis=0))
    both = dot_nn(jnp.concatenate([hi, lo], axis=0), hi_ref[...])
    total = both[:128] + (both[128:] + dot_nn(hi, lo_ref[...]))
    out_ref[:, :LAGS] = total[64:].astype(BF16)
    out_ref[:, LAGS:] = total[:64].astype(BF16)


def kernel_call(kernel, out_shape, name, args, in_hbm=(), scratch=(), cost=None, limit=24):
    vmem, hbm = pl.BlockSpec(memory_space=pltpu.VMEM), pl.BlockSpec(memory_space=pl.ANY)
    return pl.pallas_call(
        kernel,
        in_specs=[hbm if k in in_hbm else vmem for k in range(len(args))],
        out_specs=vmem,
        out_shape=out_shape,
        scratch_shapes=scratch,
        name=name,
        cost_estimate=cost,
        compiler_params=pltpu.CompilerParams(vmem_limit_bytes=limit << 20),
    )(*[pltpu.with_memory_space_constraint(a, pltpu.HBM if k in in_hbm else pltpu.VMEM) for k, a in enumerate(args)])


def body(records, fir_taps):
    forward, near, (inv_hi, inv_lo), taps_table = tables()
    y = lax.all_to_all(records, "chan", 0, 0, tiled=True, axis_index_groups=[ORDER])
    y = y.reshape(LENGTH // CHANNELS, 2 * CHANNELS, CHANNELS)
    response = jnp.dot(
        taps_table,
        jnp.broadcast_to(fir_taps[:, None], (TAPS, 128)),
        precision=lax.Precision.HIGHEST,
        preferred_element_type=F32,
    )
    even, half, odd = forward
    white = kernel_call(
        whiten_kernel,
        pltpu.VMEM((2, PER_CLASS // 8, 8, 8, CHANNELS), BF16),
        "whiten",
        (y, even, half, near, response, odd),
        in_hbm=(5,),
        scratch=[pltpu.VMEM(odd.shape, BF16), pltpu.SemaphoreType.DMA(())],
    )
    owners = BAND // 2
    white = lax.all_to_all(white.reshape(owners, 8, CHANNELS), BOTH, 0, 0, tiled=True)
    cross = kernel_call(
        cross_kernel,
        pltpu.VMEM((2 * owners, 128), F32),
        "cross",
        (white.reshape(owners // 2, 16, CHANNELS),),
        cost=pl.CostEstimate(flops=2 * 10**9, transcendentals=0, bytes_accessed=4 * 10**6),
    )
    cross = lax.all_to_all(cross.reshape(owners, 2, 128), BOTH, 0, 0, tiled=True)
    lagged = kernel_call(
        lag_kernel,
        jax.ShapeDtypeStruct((64, 2 * LAGS), BF16),
        "lag",
        (cross.reshape(2 * owners, 128), inv_hi, inv_lo),
    )
    return lagged.reshape(8, 8, 2 * LAGS)


def solution(mesh):
    in_specs = (P("win", None, "chan"), P())
    out_specs = P("chan", "win", None)
    return jax.shard_map(body, mesh=mesh, in_specs=in_specs, out_specs=out_specs, check_vma=False)
```

```python
import functools
import math

import jax
import jax.numpy as jnp
import ml_dtypes
import numpy as np
from jax import lax
from jax.experimental import pallas as pl
from jax.experimental.pallas import tpu as pltpu
from jax.sharding import PartitionSpec as P

LENGTH = 2048
BAND = 512
FIRST_BIN = 16
LAGS = 512
HALF_WIDTH = 32
TAPS = 64
CHANNELS = 128
WINDOWS = 512
BOTH = ("win", "chan")
RADIX = 4
QUARTER = LENGTH // RADIX
PER_CLASS = BAND // RADIX

ORDER = [2 * z + x for z in (0, 4, 1, 5, 2, 6, 3, 7) for x in (0, 1)]
BF16 = jnp.bfloat16
F32 = jnp.float32


def split_table(table):
    hi = table.astype(ml_dtypes.bfloat16)
    lo = (table - hi.astype(np.float64)).astype(ml_dtypes.bfloat16)
    return hi, lo


def phases(rows, cols):
    return 2.0 * math.pi / LENGTH * np.mod(rows[:, None] * cols[None, :], LENGTH).astype(np.float64)


@functools.cache
def tables():
    order = (RADIX * np.arange(PER_CLASS)[None, :] + np.arange(RADIX)[:, None]).reshape(-1)
    bins = FIRST_BIN + order
    cos, sin = (f(phases(bins, np.arange(QUARTER))).reshape(RADIX, PER_CLASS, QUARTER) for f in (np.cos, np.sin))
    even = [np.concatenate([cos[r], -sin[r]]) for r in (0, 2)]
    odd = np.concatenate(
        [
            np.concatenate([np.concatenate([cos[r], -s * sin[r]], axis=1), np.concatenate([-sin[r], -s * cos[r]], axis=1)])
            for r, s in ((1, 1), (3, -1))
        ]
    )
    forward = [np.concatenate(split_table(t)) for t in (*even, odd)]
    offset = np.mod(order[:, None] - order[None, :], BAND)
    near = (offset <= HALF_WIDTH) | (offset >= BAND - HALF_WIDTH)
    angles = phases(bins, np.arange(TAPS))
    taps = np.concatenate([np.cos(angles), -np.sin(angles)]).astype(np.float32)
    owned = order.reshape(2, 2, PER_CLASS).transpose(1, 0, 2).reshape(-1)
    angles = phases(FIRST_BIN + owned, np.arange(LAGS))
    inverse = np.stack([np.cos(angles), -np.sin(angles)], axis=1) / (WINDOWS * BAND)
    return forward, near.astype(ml_dtypes.bfloat16), split_table(inverse.reshape(2 * BAND, LAGS)), taps


def dot_nt(a, b):
    return lax.dot_general(a, b, (((1,), (1,)), ((), ())), preferred_element_type=F32)


def dot_tn(a, b):
    return lax.dot_general(a, b, (((0,), (0,)), ((), ())), preferred_element_type=F32)


def dot_nn(a, b):
    return jnp.dot(a, b, preferred_element_type=F32)


def two_terms(x):
    hi = x.astype(BF16)
    return hi, (x - hi.astype(F32)).astype(BF16)


def swap_halves(low, high, bit, shift, axis):
    size = low.shape[axis]
    new_low = jnp.where(bit, pltpu.roll(high, shift, axis), low)
    new_high = jnp.where(bit, high, pltpu.roll(low, size - shift, axis))
    return new_low, new_high


def whiten_kernel(
    y_ref, even_ref, half_ref, near_ref, resp_ref, odd_hbm, out_ref, odd_ref, sem
):
    copy = pltpu.make_async_copy(odd_hbm, odd_ref, sem)
    copy.start()
    blocks = y_ref.shape[0] // RADIX
    sums = [[], [], [], []]
    for j in range(blocks):
        u = [y_ref[ORDER.index(h * blocks + j)].astype(F32) for h in range(RADIX)]
        even, odd = u[0] + u[2], u[1] + u[3]
        for k, x in enumerate((even + odd, even - odd, u[0] - u[2], u[1] - u[3])):
            sums[k].append(two_terms(x))
    terms = [[jnp.concatenate([x[t] for x in s], axis=1) for t in range(2)] for s in sums]
    inputs = [terms[0], terms[1], [jnp.concatenate([terms[2][t], terms[3][t]], axis=1) for t in range(2)]]
    spec = [None] * 3
    for k, ref in enumerate((even_ref, half_ref, odd_ref)):
        hi, lo = inputs[k]
        rows = ref.shape[0] // 2
        if k == 2:
            copy.wait()
        both = dot_nt(ref[...], hi)
        spec[k] = both[:rows] + both[rows:] + dot_nt(ref[:rows], lo)
    m = PER_CLASS
    spec_re = jnp.concatenate([spec[0][:m], spec[2][:m], spec[1][:m], spec[2][2 * m : 3 * m]])
    spec_im = jnp.concatenate([spec[0][m:], spec[2][m : 2 * m], spec[1][m:], spec[2][3 * m :]])
    resp_re = jnp.concatenate([resp_ref[:BAND]] * 2, axis=1)
    resp_im = jnp.concatenate([resp_ref[BAND:]] * 2, axis=1)
    filt_re = spec_re * resp_re - spec_im * resp_im
    filt_im = spec_re * resp_im + spec_im * resp_re
    power = filt_re * filt_re + filt_im * filt_im
    hi, lo = two_terms(power)
    near = near_ref[...]
    smooth = (dot_nn(near, hi) + dot_nn(near, lo)) * (1.0 / (2 * HALF_WIDTH + 1))
    inv_amp = lax.rsqrt(smooth + 1e-06)
    white = (filt_re * inv_amp, filt_im * inv_amp)
    row = lax.broadcasted_iota(jnp.int32, (m, CHANNELS), 0)
    bits = [(row & s) != 0 for s in (4, 2, 1)]
    for high in range(2):
        a = []
        for k in range(8):
            r = 2 * high + k // 4
            w = k % 2
            a.append(white[k // 2 % 2][r * m : (r + 1) * m, w * CHANNELS : (w + 1) * CHANNELS])
        for bit, shift in zip(bits, (4, 2, 1)):
            for k in range(8):
                if not k & shift:
                    a[k], a[k | shift] = swap_halves(a[k], a[k | shift], bit, shift, 0)
        for k in range(8):
            out_ref[high, :, k] = a[k].reshape(m // 8, 8, CHANNELS).astype(BF16)


def cross_kernel(b_ref, out_ref):
    wide = b_ref[...].astype(F32)
    first, second = wide[:, :8], wide[:, 8:]
    bit = (lax.broadcasted_iota(jnp.int32, first.shape, 1) & 4) != 0
    imag = (lax.broadcasted_iota(jnp.int32, first.shape, 1) & 2) != 0
    parts = []
    for x in swap_halves(first, second, bit, 4, 1):
        turned = jnp.where(imag, pltpu.roll(x, 2, 1), -pltpu.roll(x, 6, 1))
        x, turned = (v.astype(BF16).reshape(-1, CHANNELS) for v in (x, turned))
        cross = dot_tn(x, jnp.concatenate([x, turned], axis=1))
        parts.append([cross[:, :CHANNELS], cross[:, CHANNELS:]])
    row = lax.broadcasted_iota(jnp.int32, (CHANNELS, CHANNELS), 0)
    lane = lax.broadcasted_iota(jnp.int32, (CHANNELS, CHANNELS), 1)
    for down, right in ((4, 32), (2, 16), (1, 8)):
        row_bit = (row & down) != 0
        lane_bit = (lane & right) != 0
        for f in range(2):
            for part in range(2):
                a = parts[f][part]
                up = pltpu.roll(pltpu.roll(a, CHANNELS - down, 0), right, 1)
                dn = pltpu.roll(pltpu.roll(a, down, 0), CHANNELS - right, 1)
                parts[f][part] = jnp.where(row_bit == lane_bit, a, jnp.where(row_bit, dn, up))
    lane_bit = (lane & 64) != 0
    for part in range(2):
        for high, a in enumerate(swap_halves(parts[0][part], parts[1][part], lane_bit, 64, 1)):
            for c in range(CHANNELS // 8):
                start = high * 256 + c * 2 + part
                out_ref[pl.ds(start, 8, stride=32), :] = a[c * 8 : c * 8 + 8]


def lag_kernel(c_ref, hi_ref, lo_ref, out_hbm, out_ref, sems):
    turned = c_ref[...].T
    c = jnp.concatenate([turned[:64], turned[64:]], axis=1)
    size = c.shape[1]
    lane = lax.broadcasted_iota(jnp.int32, c.shape, 1)
    imag = (lane & 1) != 0
    low_class = lane >= size // 2
    late = (lane & (size // 4)) != 0
    swapped = jnp.where(imag, pltpu.roll(c, 1, 1), pltpu.roll(c, size - 1, 1))
    turned = jnp.where(low_class, jnp.where(imag, -swapped, swapped), c)
    turned = jnp.where(late, -turned, turned)
    hi, lo = two_terms(jnp.concatenate([c, turned], axis=0))
    lhs = jnp.concatenate([hi, lo], axis=0)
    half = LAGS // 2
    copies = []
    for k in range(2):
        cols = pl.ds(k * half, half)
        both = dot_nn(lhs, hi_ref[:, cols])
        total = both[:128] + (both[128:] + dot_nn(hi, lo_ref[:, cols]))
        for part in range(2):
            cols = pl.ds((1 - part) * LAGS + k * half, half)
            out_ref[:, cols] = total[64 * part : 64 * part + 64].astype(BF16)
            copy = pltpu.make_async_copy(out_ref.at[:, cols], out_hbm.at[:, cols], sems.at[2 * k + part])
            copy.start()
            copies.append(copy)
    for copy in copies:
        copy.wait()


def kernel_call(kernel, out_shape, name, args, in_hbm=(), scratch=(), cost=None, limit=24, out_hbm=False):
    vmem, hbm = pl.BlockSpec(memory_space=pltpu.VMEM), pl.BlockSpec(memory_space=pl.ANY)
    return pl.pallas_call(
        kernel,
        in_specs=[hbm if k in in_hbm else vmem for k in range(len(args))],
        out_specs=hbm if out_hbm else vmem,
        out_shape=out_shape,
        scratch_shapes=scratch,
        name=name,
        cost_estimate=cost,
        compiler_params=pltpu.CompilerParams(vmem_limit_bytes=limit << 20),
    )(*[pltpu.with_memory_space_constraint(a, pltpu.HBM if k in in_hbm else pltpu.VMEM) for k, a in enumerate(args)])


def body(records, fir_taps):
    forward, near, (inv_hi, inv_lo), taps_table = tables()
    y = lax.all_to_all(records, "chan", 0, 0, tiled=True, axis_index_groups=[ORDER])
    y = y.reshape(LENGTH // CHANNELS, 2 * CHANNELS, CHANNELS)
    response = jnp.dot(
        taps_table,
        jnp.broadcast_to(fir_taps[:, None], (TAPS, 128)),
        precision=lax.Precision.HIGHEST,
        preferred_element_type=F32,
    )
    even, half, odd = forward
    white = kernel_call(
        whiten_kernel,
        pltpu.VMEM((2, PER_CLASS // 8, 8, 8, CHANNELS), BF16),
        "whiten",
        (y, even, half, near, response, odd),
        in_hbm=(5,),
        scratch=[pltpu.VMEM(odd.shape, BF16), pltpu.SemaphoreType.DMA(())],
    )
    owners = BAND // 2
    white = lax.all_to_all(white.reshape(owners, 8, CHANNELS), BOTH, 0, 0, tiled=True)
    cross = kernel_call(
        cross_kernel,
        pltpu.VMEM((2 * owners, 128), F32),
        "cross",
        (white.reshape(owners // 2, 16, CHANNELS),),
        cost=pl.CostEstimate(flops=2 * 10**9, transcendentals=0, bytes_accessed=4 * 10**6),
    )
    cross = lax.all_to_all(cross.reshape(owners, 2, 128), BOTH, 0, 0, tiled=True)
    lagged = kernel_call(
        lag_kernel,
        jax.ShapeDtypeStruct((64, 2 * LAGS), BF16),
        "lag",
        (cross.reshape(2 * owners, 128), inv_hi, inv_lo),
        scratch=[pltpu.VMEM((64, 2 * LAGS), BF16), pltpu.SemaphoreType.DMA((4,))],
        out_hbm=True,
    )
    return lagged.reshape(8, 8, 2 * LAGS)


def solution(mesh):
    in_specs = (P("win", None, "chan"), P())
    out_specs = P("chan", "win", None)
    return jax.shard_map(body, mesh=mesh, in_specs=in_specs, out_specs=out_specs, check_vma=False)
```

```python
import functools
import math

import jax
import jax.numpy as jnp
import ml_dtypes
import numpy as np
from jax import lax
from jax.experimental import pallas as pl
from jax.experimental.pallas import tpu as pltpu
from jax.sharding import PartitionSpec as P

LENGTH = 2048
BAND = 512
FIRST_BIN = 16
LAGS = 512
HALF_WIDTH = 32
TAPS = 64
CHANNELS = 128
WINDOWS = 512
BOTH = ("win", "chan")
RADIX = 4
QUARTER = LENGTH // RADIX
PER_CLASS = BAND // RADIX

ORDER = [2 * z + x for z in (0, 4, 1, 5, 2, 6, 3, 7) for x in (0, 1)]
BF16 = jnp.bfloat16
F32 = jnp.float32


def split_table(table):
    hi = table.astype(ml_dtypes.bfloat16)
    lo = (table - hi.astype(np.float64)).astype(ml_dtypes.bfloat16)
    return hi, lo


def phases(rows, cols):
    return 2.0 * math.pi / LENGTH * np.mod(rows[:, None] * cols[None, :], LENGTH).astype(np.float64)


@functools.cache
def tables():
    order = (RADIX * np.arange(PER_CLASS)[None, :] + np.arange(RADIX)[:, None]).reshape(-1)
    bins = FIRST_BIN + order
    cos, sin = (f(phases(bins, np.arange(QUARTER))).reshape(RADIX, PER_CLASS, QUARTER) for f in (np.cos, np.sin))
    even = [np.concatenate([cos[r], -sin[r]]) for r in (0, 2)]
    odd = np.concatenate(
        [
            np.concatenate([np.concatenate([cos[r], -s * sin[r]], axis=1), np.concatenate([-sin[r], -s * cos[r]], axis=1)])
            for r, s in ((1, 1), (3, -1))
        ]
    )
    forward = [np.concatenate(split_table(t)) for t in (*even, odd)]
    offset = np.mod(order[:, None] - order[None, :], BAND)
    near = (offset <= HALF_WIDTH) | (offset >= BAND - HALF_WIDTH)
    angles = phases(bins, np.arange(TAPS))
    taps = np.concatenate([np.cos(angles), -np.sin(angles)]).astype(np.float32)
    owned = order.reshape(2, 2, PER_CLASS).transpose(1, 0, 2).reshape(-1)
    angles = phases(FIRST_BIN + owned, np.arange(LAGS))
    inverse = np.stack([np.cos(angles), -np.sin(angles)], axis=1) / (WINDOWS * BAND)
    return forward, near.astype(ml_dtypes.bfloat16), split_table(inverse.reshape(2 * BAND, LAGS)), taps


def dot_nt(a, b):
    return lax.dot_general(a, b, (((1,), (1,)), ((), ())), preferred_element_type=F32)


def dot_tn(a, b):
    return lax.dot_general(a, b, (((0,), (0,)), ((), ())), preferred_element_type=F32)


def dot_nn(a, b):
    return jnp.dot(a, b, preferred_element_type=F32)


def two_terms(x):
    hi = x.astype(BF16)
    return hi, (x - hi.astype(F32)).astype(BF16)


def swap_halves(low, high, bit, shift, axis):
    size = low.shape[axis]
    new_low = jnp.where(bit, pltpu.roll(high, shift, axis), low)
    new_high = jnp.where(bit, high, pltpu.roll(low, size - shift, axis))
    return new_low, new_high


def whiten_kernel(
    y_ref, even_ref, half_ref, near_ref, resp_ref, odd_hbm, out_ref, odd_ref, sem
):
    part = odd_ref.shape[0] // 2
    copies = [
        pltpu.make_async_copy(odd_hbm.at[pl.ds(k * part, part)], odd_ref.at[pl.ds(k * part, part)], sem.at[k])
        for k in range(2)
    ]
    for copy in copies:
        copy.start()
    blocks = y_ref.shape[0] // RADIX
    sums = [[], [], [], []]
    for j in range(blocks):
        u = [y_ref[ORDER.index(h * blocks + j)].astype(F32) for h in range(RADIX)]
        even, odd = u[0] + u[2], u[1] + u[3]
        for k, x in enumerate((even + odd, even - odd, u[0] - u[2], u[1] - u[3])):
            sums[k].append(two_terms(x))
    terms = [[jnp.concatenate([x[t] for x in s], axis=1) for t in range(2)] for s in sums]
    inputs = [terms[0], terms[1], [jnp.concatenate([terms[2][t], terms[3][t]], axis=1) for t in range(2)]]
    spec = [None] * 3
    for k, ref in enumerate((even_ref, half_ref, odd_ref)):
        hi, lo = inputs[k]
        rows = ref.shape[0] // 2
        if k == 2:
            copies[0].wait()
            first = dot_nt(ref[:rows], hi) + dot_nt(ref[:rows], lo)
            copies[1].wait()
            spec[k] = first + dot_nt(ref[rows:], hi)
        else:
            both = dot_nt(ref[...], hi)
            spec[k] = both[:rows] + both[rows:] + dot_nt(ref[:rows], lo)
    m = PER_CLASS
    spec_re = jnp.concatenate([spec[0][:m], spec[2][:m], spec[1][:m], spec[2][2 * m : 3 * m]])
    spec_im = jnp.concatenate([spec[0][m:], spec[2][m : 2 * m], spec[1][m:], spec[2][3 * m :]])
    resp_re = jnp.concatenate([resp_ref[:BAND]] * 2, axis=1)
    resp_im = jnp.concatenate([resp_ref[BAND:]] * 2, axis=1)
    filt_re = spec_re * resp_re - spec_im * resp_im
    filt_im = spec_re * resp_im + spec_im * resp_re
    power = filt_re * filt_re + filt_im * filt_im
    hi, lo = two_terms(power)
    near = near_ref[...]
    smooth = (dot_nn(near, hi) + dot_nn(near, lo)) * (1.0 / (2 * HALF_WIDTH + 1))
    inv_amp = lax.rsqrt(smooth + 1e-06)
    white = (filt_re * inv_amp, filt_im * inv_amp)
    row = lax.broadcasted_iota(jnp.int32, (m, CHANNELS), 0)
    bits = [(row & s) != 0 for s in (4, 2, 1)]
    for high in range(2):
        a = []
        for k in range(8):
            r = 2 * high + k // 4
            w = k % 2
            a.append(white[k // 2 % 2][r * m : (r + 1) * m, w * CHANNELS : (w + 1) * CHANNELS])
        for bit, shift in zip(bits, (4, 2, 1)):
            for k in range(8):
                if not k & shift:
                    a[k], a[k | shift] = swap_halves(a[k], a[k | shift], bit, shift, 0)
        for k in range(8):
            out_ref[high, :, k] = a[k].reshape(m // 8, 8, CHANNELS).astype(BF16)


def cross_kernel(b_ref, out_ref):
    wide = b_ref[...].astype(F32)
    first, second = wide[:, :8], wide[:, 8:]
    bit = (lax.broadcasted_iota(jnp.int32, first.shape, 1) & 4) != 0
    imag = (lax.broadcasted_iota(jnp.int32, first.shape, 1) & 2) != 0
    parts = []
    for x in swap_halves(first, second, bit, 4, 1):
        turned = jnp.where(imag, pltpu.roll(x, 2, 1), -pltpu.roll(x, 6, 1))
        x, turned = (v.astype(BF16).reshape(-1, CHANNELS) for v in (x, turned))
        cross = dot_tn(x, jnp.concatenate([x, turned], axis=1))
        parts.append([cross[:, :CHANNELS], cross[:, CHANNELS:]])
    row = lax.broadcasted_iota(jnp.int32, (CHANNELS, CHANNELS), 0)
    lane = lax.broadcasted_iota(jnp.int32, (CHANNELS, CHANNELS), 1)
    for down, right in ((4, 32), (2, 16), (1, 8)):
        row_bit = (row & down) != 0
        lane_bit = (lane & right) != 0
        for f in range(2):
            for part in range(2):
                a = parts[f][part]
                up = pltpu.roll(pltpu.roll(a, CHANNELS - down, 0), right, 1)
                dn = pltpu.roll(pltpu.roll(a, down, 0), CHANNELS - right, 1)
                parts[f][part] = jnp.where(row_bit == lane_bit, a, jnp.where(row_bit, dn, up))
    lane_bit = (lane & 64) != 0
    for part in range(2):
        for high, a in enumerate(swap_halves(parts[0][part], parts[1][part], lane_bit, 64, 1)):
            for c in range(CHANNELS // 8):
                start = high * 256 + c * 2 + part
                out_ref[pl.ds(start, 8, stride=32), :] = a[c * 8 : c * 8 + 8]


def lag_kernel(c_ref, hi_ref, lo_ref, out_ref):
    c = c_ref[...]
    rows = c.shape[0]
    row = lax.broadcasted_iota(jnp.int32, c.shape, 0)
    imag = (row & 1) != 0
    late = row >= rows // 2
    low_class = lax.broadcasted_iota(jnp.int32, c.shape, 1) >= c.shape[1] // 2
    swapped = jnp.where(imag, pltpu.roll(c, 1, 0), pltpu.roll(c, rows - 1, 0))
    turned = jnp.where(low_class, jnp.where(imag, -swapped, swapped), c)
    turned = jnp.where(late, -turned, turned)
    halves = []
    for x in (c.T, turned.T):
        halves.append(jnp.concatenate([x[:64], x[64:]], axis=1))
    hi, lo = two_terms(jnp.concatenate(halves, axis=0))
    both = dot_nn(jnp.concatenate([hi, lo], axis=0), hi_ref[...])
    total = both[:128] + (both[128:] + dot_nn(hi, lo_ref[...]))
    out_ref[:, :LAGS] = total[64:].astype(BF16)
    out_ref[:, LAGS:] = total[:64].astype(BF16)


def kernel_call(kernel, out_shape, name, args, in_hbm=(), scratch=(), cost=None, limit=24):
    vmem, hbm = pl.BlockSpec(memory_space=pltpu.VMEM), pl.BlockSpec(memory_space=pl.ANY)
    return pl.pallas_call(
        kernel,
        in_specs=[hbm if k in in_hbm else vmem for k in range(len(args))],
        out_specs=vmem,
        out_shape=out_shape,
        scratch_shapes=scratch,
        name=name,
        cost_estimate=cost,
        compiler_params=pltpu.CompilerParams(vmem_limit_bytes=limit << 20),
    )(*[pltpu.with_memory_space_constraint(a, pltpu.HBM if k in in_hbm else pltpu.VMEM) for k, a in enumerate(args)])


def body(records, fir_taps):
    forward, near, (inv_hi, inv_lo), taps_table = tables()
    y = lax.all_to_all(records, "chan", 0, 0, tiled=True, axis_index_groups=[ORDER])
    y = y.reshape(LENGTH // CHANNELS, 2 * CHANNELS, CHANNELS)
    response = jnp.dot(
        taps_table,
        jnp.broadcast_to(fir_taps[:, None], (TAPS, 128)),
        precision=lax.Precision.HIGHEST,
        preferred_element_type=F32,
    )
    even, half, odd = forward
    white = kernel_call(
        whiten_kernel,
        pltpu.VMEM((2, PER_CLASS // 8, 8, 8, CHANNELS), BF16),
        "whiten",
        (y, even, half, near, response, odd),
        in_hbm=(5,),
        scratch=[pltpu.VMEM(odd.shape, BF16), pltpu.SemaphoreType.DMA((2,))],
    )
    owners = BAND // 2
    white = lax.all_to_all(white.reshape(owners, 8, CHANNELS), BOTH, 0, 0, tiled=True)
    cross = kernel_call(
        cross_kernel,
        pltpu.VMEM((2 * owners, 128), F32),
        "cross",
        (white.reshape(owners // 2, 16, CHANNELS),),
        cost=pl.CostEstimate(flops=2 * 10**9, transcendentals=0, bytes_accessed=4 * 10**6),
    )
    cross = lax.all_to_all(cross.reshape(owners, 2, 128), BOTH, 0, 0, tiled=True)
    lagged = kernel_call(
        lag_kernel,
        jax.ShapeDtypeStruct((64, 2 * LAGS), BF16),
        "lag",
        (cross.reshape(2 * owners, 128), inv_hi, inv_lo),
    )
    return lagged.reshape(8, 8, 2 * LAGS)


def solution(mesh):
    in_specs = (P("win", None, "chan"), P())
    out_specs = P("chan", "win", None)
    return jax.shard_map(body, mesh=mesh, in_specs=in_specs, out_specs=out_specs, check_vma=False)
```
